512 devices in a mesh: ap: 32 (over x, y), pass: 16 (over z, core).
Axes of the slice: x: 4, y: 8, z: 8, core: 2. Of those that a mesh axis runs over, the one named last changes fastest.
Arguments:
- echo: bfloat16 [16, 256, 2, 3072], P('pass', 'ap'), may hold values from -6 to 6
- chirp: bfloat16 [2, 1024], replicated, may hold values from -0.125 to 0.125
- pair_swap: int32 [16, 8], P('pass'), may hold values from 0 to 1
- range_shift: int32 [16, 8, 2], P('pass'), may hold values from -16 to 16, as said below
- angle_shift: int32 [16, 8, 2, 2], P('pass'), may hold values from -3 to 3, as said below
- range_taps: float32 [8, 2, 8], replicated, may hold values from -2 to 2
- angle_taps: float32 [8, 2, 2, 8], replicated, may hold values from -2 to 2
- phase_rates: float32 [8, 2, 2, 2], replicated, may hold values from -3.140625 to 3.140625
- invert: float32 [2, 64, 32], replicated, may hold values from -1 to 1
- baseline_index: int32 [16], replicated, may hold values from 0 to 31
Outputs:
- tomogram: float32 [16, 64, 32, 1024], P('pass', None, 'ap')
The draws below stay inside these ranges and needn't reach their ends.
Inputs may be any that keep to these rules, and one draw needn't show every extreme that they name: `range_shift`: both 16 and -16 occur. `angle_shift`: both 3 and -3 occur.
All inputs are finite; a program needn't handle non-finite values.
Results may differ from the reference program's by a relative error of at most 0.0003.
Values sent between devices are 32-bit elements; how exact they have to be, the bound alone decides.
No kernel may reach another device: no remote copies, remote signals or barrier semaphores. Data moves between devices by JAX's collectives and lax.ppermute only.
A program may use at most 64 MiB of HBM per device.

```python
import math
import jax
import jax.numpy as jnp
from jax import lax

NR = 2048
TAPS = 1024
HEIGHTS = 64
KT = 8
RMAX = 16
AMAX = 3
BASES = 32
NS = 3072
PULSES = 256
PASSES = 16
RW = 64
XLEV = 5
LEVELS = 8
RLEV = 8
N_AP = 32


def draw_extremes(key, layout, extreme):
    entries = math.prod(layout)
    values = jax.random.randint(key, (entries,), -extreme, extreme + 1, dtype=jnp.int32)
    shuffled = jax.random.permutation(jax.random.fold_in(key, 7), entries)
    values = values.at[shuffled[0]].set(extreme).at[shuffled[1]].set(-extreme)
    return values.reshape(layout)


def draw_range_shift(key, part):
    return draw_extremes(jax.random.fold_in(key, 11), (PASSES, RLEV, 2), RMAX)


def draw_angle_shift(key, part):
    return draw_extremes(jax.random.fold_in(key, 13), (PASSES, LEVELS, 2, 2), AMAX)


def place_ends(array, stream_key, smallest, high):
    dims = array.shape
    index_at = [jax.random.randint(jax.random.fold_in(stream_key, axis), (), 0, dims[axis]) for axis in range(len(dims))]
    array = array.at[tuple(index_at)].set(smallest)
    longest = dims.index(max(dims))
    index_at[longest] = (index_at[longest] + 1) % dims[longest]
    return array.at[tuple(index_at)].set(high)


def block_levels(own_key, shape, cuts, least, top_value):
    def one(axis_at, parts):
        heights = jax.random.uniform(jax.random.fold_in(jax.random.fold_in(own_key, 6), axis_at), (parts,), jnp.float32, least / len(cuts), top_value / len(cuts))
        return jnp.repeat(jnp.exp(heights), shape[axis_at] // parts).reshape((-1,) + (1,) * (len(shape) - axis_at - 1))

    factor_of = one(*cuts[0])
    for cut in cuts[1:]:
        factor_of = factor_of * one(*cut)
    return factor_of


def gaussian(stream_key, dims, scale, limit, cuts=(), held_as=jnp.bfloat16):
    array = scale * jax.random.normal(stream_key, dims, jnp.float32)
    if cuts:
        array = array * block_levels(stream_key, dims, cuts, -0.22, 0.18)
    return jnp.clip(array, -limit, limit).astype(held_as)


def setup_inputs(seed: int = 0) -> dict:
    key_list = jax.random.split(jax.random.key(seed), 11)
    echo = gaussian(key_list[0], (PASSES, PULSES, 2, NS), 1.0, 6.0, ((0, 16), (1, 32)))
    chirp = gaussian(key_list[1], (2, TAPS), (2 * TAPS) ** -0.5, 0.125)
    pair_swap = place_ends(jax.random.randint(key_list[2], (PASSES, LEVELS), 0, 2), jax.random.fold_in(key_list[2], 1), 0, 1).astype(jnp.int32)
    range_shift = draw_range_shift(jax.random.fold_in(key_list[10], 71), 0)
    angle_shift = draw_angle_shift(jax.random.fold_in(key_list[10], 71), 0)
    range_taps = gaussian(key_list[5], (RLEV, 2, KT), KT ** -0.5, 2.0, (), jnp.float32)
    angle_taps = gaussian(key_list[6], (LEVELS, 2, 2, KT), KT ** -0.5, 2.0, (), jnp.float32)
    phase_rates = jnp.clip(jax.random.uniform(key_list[7], (LEVELS, 2, 2, 2), jnp.float32, -3.140625, 3.140625), -3.140625, 3.140625)
    invert = gaussian(key_list[8], (2, HEIGHTS, BASES), (2 * PASSES) ** -0.5, 1.0, (), jnp.float32)
    baseline_index = place_ends(jax.random.randint(key_list[9], (PASSES,), 0, BASES), jax.random.fold_in(key_list[9], 1), 0, BASES - 1).astype(jnp.int32)
    return dict(echo=echo, chirp=chirp, pair_swap=pair_swap, range_shift=range_shift, angle_shift=angle_shift, range_taps=range_taps, angle_taps=angle_taps, phase_rates=phase_rates, invert=invert, baseline_index=baseline_index)


SQRT_HALF = math.sqrt(0.5)

def interp(values, tap_row, offset, along, margin, fill_mode):
    length = values.shape[along]
    widths = [(0, 0)] * values.ndim
    widths[along] = (margin, margin)
    padded = jnp.pad(values, widths, mode=fill_mode)
    summed = jnp.zeros_like(values)
    for position in range(tap_row.shape[0]):
        begin_at = margin + position - (KT // 2 - 1) + offset
        summed = summed + tap_row[position] * lax.dynamic_slice_in_dim(padded, begin_at, length, along)
    return summed

def merge_pair(first, second, section_index, flip, range_row, angle_row, range_taps, angle_taps, phase_rates, r_frac, j_grid, beam_axis, range_axis, trim):
    beams = first.shape[beam_axis]
    prepared = []
    for c, child in enumerate((first, second)):
        role_index = (c + flip) % 2
        child = interp(child, range_taps[section_index, role_index], range_row[section_index, role_index], range_axis, RMAX + KT, 'constant')
        if trim > 0:
            child = lax.slice_in_dim(child, trim, child.shape[range_axis] - trim, axis=range_axis)
        prepared.append((child, role_index))
    results = []
    for h in range(2):
        terms = []
        for child, role_index in prepared:
            steered = interp(child, angle_taps[section_index, role_index, h], angle_row[section_index, role_index, h], beam_axis, AMAX + KT, 'edge')
            rates = phase_rates[section_index, role_index, h]
            phase = 8.0 * (rates[0] * r_frac + rates[1] * ((2.0 * j_grid + h) / (2.0 * beams)))
            cosine = jnp.cos(phase)
            sine = jnp.sin(phase)
            terms.append(jnp.stack([cosine * steered[0] - sine * steered[1], sine * steered[0] + cosine * steered[1]], 0))
        results.append((terms[0] + terms[1]) * SQRT_HALF)
    stacked = jnp.stack(results, axis=beam_axis + 1)
    new_shape = list(results[0].shape)
    new_shape[beam_axis] = 2 * beams
    return stacked.reshape(new_shape)

def reference(echo, chirp, pair_swap, range_shift, angle_shift, range_taps, angle_taps, phase_rates, invert, baseline_index):
    window = jnp.arange(NS)[:, None] - jnp.arange(NR)[None, :]
    inside = (window >= 0) & (window < TAPS)
    clipped = jnp.clip(window, 0, TAPS - 1)
    chirp_wide = chirp.astype(jnp.float32)
    real_kernel = jnp.where(inside, chirp_wide[0][clipped], 0.0)
    imag_kernel = jnp.where(inside, chirp_wide[1][clipped], 0.0)
    highest = lax.Precision.HIGHEST

    def one_pass(inputs):
        echo_pass, swap_row, range_row, angle_row = inputs
        real_echo = echo_pass[:, 0].astype(jnp.float32)
        imag_echo = echo_pass[:, 1].astype(jnp.float32)
        real_out = jnp.dot(real_echo, real_kernel, precision=highest, preferred_element_type=jnp.float32) + jnp.dot(imag_echo, imag_kernel, precision=highest, preferred_element_type=jnp.float32)
        imag_out = jnp.dot(imag_echo, real_kernel, precision=highest, preferred_element_type=jnp.float32) - jnp.dot(real_echo, imag_kernel, precision=highest, preferred_element_type=jnp.float32)
        image = jnp.stack([real_out, imag_out], 0).reshape(2, PULSES, 1, NR)
        r_frac = (jnp.arange(NR, dtype=jnp.float32) / NR)[None, :]
        for section_index in range(LEVELS):
            groups = image.shape[1]
            beams = image.shape[2]
            pairs = image.reshape(2, groups // 2, 2, beams, NR)
            j_grid = jnp.arange(beams, dtype=jnp.float32)[:, None]
            image = merge_pair(pairs[:, :, 0], pairs[:, :, 1], section_index, swap_row[section_index], range_row, angle_row, range_taps, angle_taps, phase_rates, r_frac, j_grid, 2, 3, 0)
        return image[:, 0]
    images = lax.map(one_pass, (echo, pair_swap, range_shift, angle_shift))
    steer = invert[:, :, baseline_index]

    def one_block(block_index):
        reversed_index = jnp.zeros((), jnp.int32)
        for digit in range(XLEV):
            reversed_index = reversed_index + block_index // 2 ** digit % 2 * 2 ** (XLEV - 1 - digit)
        piece = lax.dynamic_slice_in_dim(images, (reversed_index * RW).astype(jnp.int32), RW, 3)
        real_sum = jnp.einsum('hp,pqr->hrq', steer[0], piece[:, 0], precision=highest) - jnp.einsum('hp,pqr->hrq', steer[1], piece[:, 1], precision=highest)
        imag_sum = jnp.einsum('hp,pqr->hrq', steer[1], piece[:, 0], precision=highest) + jnp.einsum('hp,pqr->hrq', steer[0], piece[:, 1], precision=highest)
        return real_sum * real_sum + imag_sum * imag_sum
    blocks = lax.map(one_block, jnp.arange(N_AP, dtype=jnp.int32))
    per_pass = PULSES // PASSES
    split = blocks.reshape(N_AP, HEIGHTS, RW, PASSES, per_pass)
    return jnp.transpose(split, (3, 1, 0, 2, 4)).reshape(PASSES, HEIGHTS, N_AP, RW * per_pass)
```

```python
import math

import jax
import jax.numpy as jnp
from jax import lax
from jax.experimental import pallas as pl
from jax.experimental.pallas import tpu as pltpu
from jax.sharding import PartitionSpec as P

NR = 2048
TAPS = 1024
NS = 3072
HEIGHTS = 64
KT = 8
ORIGIN = KT // 2 - 1
BASES = 32
LEVELS = 8
LOCAL = 3
CROSS = 5
PULSES = 8
N_AP = 32
PASSES = 16
RW = 64
BEAMS = 256
LANES = 128
TILES = 17
WINDOW = TAPS + LANES
SQRT_HALF = math.sqrt(0.5)
F32 = jnp.float32
BF16 = jnp.bfloat16

ROWS = (96, 88, 80, 72, 64)


def iota(shape, dim):
    return lax.broadcasted_iota(jnp.int32, shape, dim)


def sincos(x):
    turns = jnp.floor(x * (2.0 / math.pi) + 0.5)
    quadrant = turns.astype(jnp.int32)
    y = x - turns * 1.5703125
    y = y - turns * 4.837512969970703e-4
    y = y - turns * 7.54978995489188e-8
    y2 = y * y
    s = y * (1.0 + y2 * (-1.6666654611e-1 + y2 * (8.3321608736e-3 + y2 * -1.9515295891e-4)))
    c = 1.0 - 0.5 * y2 + y2 * y2 * (4.166664568298827e-2 + y2 * (-1.388731625493765e-3 + y2 * 2.443315711809948e-5))
    swap = (quadrant & 1) == 1
    cos_abs = jnp.where(swap, s, c)
    sin_abs = jnp.where(swap, c, s)
    cos = jnp.where(((quadrant + 1) & 2) == 2, -cos_abs, cos_abs)
    sin = jnp.where((quadrant & 2) == 2, -sin_abs, sin_abs)
    return cos, sin


def complex_mul(ar, ai, br, bi):
    return ar * br - ai * bi, ar * bi + ai * br


def reverse_bits(value):
    result = 0
    for digit in range(CROSS):
        result = result + (value // 2**digit % 2) * 2 ** (CROSS - 1 - digit)
    return result


def role(swap_ref, level, child):
    flip = swap_ref[0, level]
    return flip if child == 0 else 1 - flip


def step_offset(swap_ref, shift_ref, level, child):
    return shift_ref[0, level, role(swap_ref, level, child)] - ORIGIN


def compress_kernel(
    echo_ref,
    chirp_ref,
    swap_ref,
    range_shift_ref,
    angle_shift_ref,
    range_taps_ref,
    angle_taps_ref,
    rates_ref,
    out_ref,
    echo_rows,
    shifted,
    product,
    images,
):
    position = lax.axis_index("ap")

    offset_above = jnp.int32(0)
    for level in range(LOCAL, LEVELS):
        bit = position // 2 ** (level - LOCAL) % 2
        offset_above = offset_above + jnp.where(
            bit == 1,
            step_offset(swap_ref, range_shift_ref, level, 1),
            step_offset(swap_ref, range_shift_ref, level, 0),
        )
    local_steps = [
        [step_offset(swap_ref, range_shift_ref, level, child) for child in range(2)]
        for level in range(LOCAL)
    ]

    tiles_in = NS // LANES
    tiles_out = TILES + WINDOW // LANES
    lane = iota((2, LANES), 1)
    echo_rows[:, :2] = jnp.zeros((PULSES, 2, 2, LANES), F32)
    echo_rows[:, 2 + tiles_in :] = jnp.zeros((PULSES, 3, 2, LANES), F32)
    for n in range(PULSES):
        total = offset_above
        for level in range(LOCAL):
            total = total + local_steps[level][n >> level & 1]
        whole = total >> 7
        rest = total & (LANES - 1)
        pulse = echo_ref[0, n].astype(F32)
        for t in range(tiles_in):
            echo_rows[n, 2 + t] = pltpu.roll(
                pulse[:, t * LANES : (t + 1) * LANES], (LANES - rest) & (LANES - 1), 1
            )
        keep = lane < LANES - rest
        for t in range(tiles_out):
            index = jnp.clip(t + 2 + whole, 0, tiles_in + 3)
            left = echo_rows[n, index]
            right = echo_rows[n, index + 1]
            shifted[2 * n : 2 * n + 2, t * LANES : (t + 1) * LANES] = jnp.where(keep, left, right)

    signal = shifted[...].astype(BF16)
    windows = jnp.concatenate(
        [signal[:, b * LANES : b * LANES + WINDOW] for b in range(TILES)], axis=0
    )
    bands = []
    row = iota((LANES, LANES), 0)
    column = iota((LANES, LANES), 1)
    for part in range(2):
        previous = jnp.zeros((LANES, LANES), F32)
        pieces = []
        for t in range(WINDOW // LANES):
            if t * LANES < TAPS:
                samples = chirp_ref[part : part + 1, t * LANES : (t + 1) * LANES].astype(F32)
                current = pltpu.roll(
                    jnp.broadcast_to(samples, (LANES, LANES)), 0, 1, stride=1, stride_axis=0
                )
            else:
                current = jnp.zeros((LANES, LANES), F32)
            pieces.append(jnp.where(column >= row, current, previous).astype(BF16))
            previous = current
        bands.append(jnp.concatenate(pieces, axis=1))
    banded = jnp.concatenate(bands, axis=0)
    correlated = lax.dot_general(
        windows, banded, (((1,), (1,)), ((), ())), preferred_element_type=F32
    )
    for part in range(2):
        product[part] = correlated[:, part * LANES : (part + 1) * LANES]

    rows8 = iota((PULSES, LANES), 0)
    lanes8 = iota((PULSES, LANES), 1)

    def row_offset(first_level):
        total = jnp.full((PULSES, LANES), offset_above, jnp.int32)
        for level in range(first_level, LOCAL):
            bit = rows8 >> level & 1
            total = total + jnp.where(bit == 1, local_steps[level][1], local_steps[level][0])
        return total

    cell = row_offset(0) + lanes8
    for b in range(TILES):
        even, odd = (
            [product[part, pl.ds(16 * b + i, PULSES, stride=2), :] for part in range(2)]
            for i in range(2)
        )
        where_r = cell + b * LANES
        inside = (where_r >= 0) & (where_r < NR)
        images[0, 0, b] = jnp.where(inside, even[0] + odd[1], 0.0)
        images[0, 1, b] = jnp.where(inside, odd[0] - even[1], 0.0)
    images[:, :, TILES] = jnp.zeros((2, 2, PULSES, LANES), F32)

    for level in range(LOCAL):
        source, target = level % 2, 1 - level % 2
        beams = 2**level
        in_child = rows8 >> level & 1
        tap_rows = [
            jnp.where(
                in_child == 1,
                range_taps_ref[level, role(swap_ref, level, 1), u],
                range_taps_ref[level, role(swap_ref, level, 0), u],
            )
            for u in range(KT)
        ]
        parity = rows8 & 1
        beam = rows8 % (2 * beams) // 2
        group = rows8 // (2 * beams)
        offset_out = row_offset(level + 1)
        beam_fraction = (rows8 % (2 * beams)).astype(F32) / (2.0 * beams)
        weights = []
        waves = []
        steps = []
        for child in range(2):
            e = role(swap_ref, level, child)
            shift = jnp.where(
                parity == 1, angle_shift_ref[0, level, e, 1], angle_shift_ref[0, level, e, 0]
            )
            columns = [jnp.zeros((PULSES, LANES), F32) for _ in range(beams)]
            for u in range(KT):
                tap = jnp.where(
                    parity == 1, angle_taps_ref[level, e, 1, u], angle_taps_ref[level, e, 0, u]
                )
                picked = jnp.clip(beam + (u - ORIGIN) + shift, 0, beams - 1)
                for k in range(beams):
                    columns[k] = columns[k] + jnp.where(picked == k, tap, 0.0)
            weights.append(columns)
            slope = jnp.where(parity == 1, rates_ref[level, e, 1, 0], rates_ref[level, e, 0, 0])
            bend = jnp.where(parity == 1, rates_ref[level, e, 1, 1], rates_ref[level, e, 0, 1])
            slope = slope * (8.0 / NR)
            cos, sin = sincos(
                slope * (offset_out + lanes8).astype(F32) + 8.0 * (bend * beam_fraction)
            )
            waves.append((cos * SQRT_HALF, sin * SQRT_HALF))
            steps.append(sincos(slope * float(LANES)))
        cell_out = offset_out + lanes8
        for b in range(TILES):
            ranged = []
            for part in range(2):
                here = images[source, part, b]
                there = images[source, part, b + 1]
                total = tap_rows[0] * here
                for u in range(1, KT):
                    moved = jnp.where(
                        lanes8 < LANES - u,
                        pltpu.roll(here, LANES - u, 1),
                        pltpu.roll(there, LANES - u, 1),
                    )
                    total = total + tap_rows[u] * moved
                ranged.append(total)
            out_real = jnp.zeros((PULSES, LANES), F32)
            out_imag = jnp.zeros((PULSES, LANES), F32)
            for child in range(2):
                steered = []
                for part in range(2):
                    total = jnp.zeros((PULSES, LANES), F32)
                    for k in range(beams):
                        spread = jnp.broadcast_to(
                            ranged[part][child * beams + k : child * beams + k + 1], (PULSES, LANES)
                        )
                        for g in range(1, PULSES // (2 * beams)):
                            at = (2 * g + child) * beams + k
                            spread = jnp.where(
                                group == g,
                                jnp.broadcast_to(ranged[part][at : at + 1], (PULSES, LANES)),
                                spread,
                            )
                        total = total + weights[child][k] * spread
                    steered.append(total)
                real, imag = complex_mul(*waves[child], *steered)
                out_real = out_real + real
                out_imag = out_imag + imag
                waves[child] = complex_mul(*waves[child], *steps[child])
            where_r = cell_out + b * LANES
            inside = (where_r >= 0) & (where_r < NR)
            images[target, 0, b] = jnp.where(inside, out_real, 0.0)
            images[target, 1, b] = jnp.where(inside, out_imag, 0.0)

    last = LOCAL % 2
    for block in range(N_AP):
        start = reverse_bits(block) * RW
        t = start // LANES
        for part in range(2):
            if start % LANES == 0:
                value = images[last, part, t]
            else:
                value = jnp.where(
                    lanes8 < RW,
                    pltpu.roll(images[last, part, t], RW, 1),
                    pltpu.roll(images[last, part, t + 1], RW, 1),
                )
            out_ref[block, part * PULSES : (part + 1) * PULSES, :] = value


def merge_kernel(
    blocks_ref,
    swap_ref,
    range_shift_ref,
    angle_shift_ref,
    range_taps_ref,
    angle_taps_ref,
    rates_ref,
    out_ref,
    images,
    final,
):
    position = lax.axis_index("ap")
    base = reverse_bits(position) * RW
    half = LANES

    for child in range(2):
        order = []
        for i in range(N_AP // 2):
            order.append(
                child + 2 * (i >> 3 & 1) + 4 * (i >> 2 & 1) + 8 * (i >> 1 & 1) + 16 * (i & 1)
            )
        for part in range(2):
            stacked = jnp.concatenate(
                [blocks_ref[g, part * PULSES : (part + 1) * PULSES, :] for g in order], axis=0
            )
            images[0, child, part] = stacked.T

    column = iota((1, 2 * half), 1)
    row = iota((half, 2 * half), 0)
    for k in range(CROSS):
        level = LOCAL + k
        beams = 2**level
        rows = ROWS[k]
        source, target = k % 2, 1 - k % 2
        last = k == CROSS - 1
        parity = column & 1
        beam = column % (2 * beams) // 2
        first_row = column // (2 * beams) * beams
        beam_fraction = (column % (2 * beams)).astype(F32) / (2.0 * beams)
        offset = jnp.zeros((1, 2 * half), jnp.int32)
        for later in range(level + 1, LEVELS):
            digit = later - level - 1
            bit = column >> (7 - digit) & 1
            offset = offset + jnp.where(
                bit == 1,
                step_offset(swap_ref, range_shift_ref, later, 1),
                step_offset(swap_ref, range_shift_ref, later, 0),
            )
        cell = iota((8, 2 * half), 0) + (base + offset)
        steered = []
        waves = []
        steps = []
        for child in range(2):
            e = role(swap_ref, level, child)
            parts = []
            for part in range(2):
                total = range_taps_ref[level, e, 0] * images[source, child, part, 0:rows, :]
                for u in range(1, KT):
                    total = total + (
                        range_taps_ref[level, e, u] * images[source, child, part, u : u + rows, :]
                    )
                parts.append(total)
            ranged = jnp.concatenate(parts, axis=0)
            high = ranged.astype(BF16)
            low = (ranged - high.astype(F32)).astype(BF16)

            shift = jnp.where(
                parity == 1, angle_shift_ref[0, level, e, 1], angle_shift_ref[0, level, e, 0]
            )
            weights = jnp.zeros((half, 2 * half), F32)
            for u in range(KT):
                tap = jnp.where(
                    parity == 1, angle_taps_ref[level, e, 1, u], angle_taps_ref[level, e, 0, u]
                )
                picked = first_row + jnp.clip(beam + (u - ORIGIN) + shift, 0, beams - 1)
                weights = weights + jnp.where(row == picked, tap, 0.0)
            weights_high = weights.astype(BF16)
            weights_low = (weights - weights_high.astype(F32)).astype(BF16)
            steered.append(
                jnp.dot(
                    jnp.concatenate([high, low, high], axis=1),
                    jnp.concatenate([weights_high, weights_high, weights_low], axis=0),
                    preferred_element_type=F32,
                )
            )
            slope = jnp.where(parity == 1, rates_ref[level, e, 1, 0], rates_ref[level, e, 0, 0])
            bend = jnp.where(parity == 1, rates_ref[level, e, 1, 1], rates_ref[level, e, 0, 1])
            slope = slope * (8.0 / NR)
            cos, sin = sincos(slope * cell.astype(F32) + 8.0 * (bend * beam_fraction))
            waves.append((cos * SQRT_HALF, sin * SQRT_HALF))
            steps.append(sincos(jnp.broadcast_to(slope * 8.0, (8, 2 * half))))
        for m in range(rows // 8):
            out_real = jnp.zeros((8, 2 * half), F32)
            out_imag = jnp.zeros((8, 2 * half), F32)
            for child in range(2):
                real, imag = complex_mul(
                    *waves[child],
                    steered[child][8 * m : 8 * m + 8],
                    steered[child][rows + 8 * m : rows + 8 * m + 8],
                )
                out_real = out_real + real
                out_imag = out_imag + imag
                waves[child] = complex_mul(*waves[child], *steps[child])
            if last:
                for part, value in enumerate((out_real, out_imag)):
                    for side in range(2):
                        final[part, side, 8 * m : 8 * m + 8] = value[
                            :, side * half : (side + 1) * half
                        ]
            else:
                where_r = cell + 8 * m
                inside = (where_r >= 0) & (where_r < NR)
                for part, value in enumerate((out_real, out_imag)):
                    value = jnp.where(inside, value, 0.0)
                    for child in range(2):
                        images[target, child, part, 8 * m : 8 * m + 8, :] = value[
                            :, child * half : (child + 1) * half
                        ]

    block_of = iota((8, LANES), 1) // 16
    for part in range(2):
        for side in range(2):
            values = [final[part, side, pl.ds(i, 8, stride=8), :] for i in range(8)]
            for d in (4, 2, 1):
                clear = (block_of & d) == 0
                for i in range(8):
                    if i & d == 0:
                        a, b = values[i], values[i | d]
                        values[i] = jnp.where(clear, a, pltpu.roll(b, 16 * d, 1))
                        values[i | d] = jnp.where(clear, pltpu.roll(a, LANES - 16 * d, 1), b)
            for q in range(8):
                out_ref[side * 8 + q, part * 8 : part * 8 + 8, :] = values[q]


def invert_kernel(data_ref, invert_ref, baseline_ref, out_ref):
    column = iota((1, 2 * PASSES), 1)
    wanted = jnp.zeros((1, 2 * PASSES), jnp.int32)
    for p in range(PASSES):
        wanted = jnp.where(column // 2 == p, baseline_ref[p], wanted)
    chosen = (iota((BASES, 2 * PASSES), 0) == wanted).astype(F32)
    highest = lax.Precision.HIGHEST
    steer_real = jnp.dot(invert_ref[0], chosen, precision=highest, preferred_element_type=F32)
    steer_imag = jnp.dot(invert_ref[1], chosen, precision=highest, preferred_element_type=F32)
    imaginary = (iota((HEIGHTS, 2 * PASSES), 1) & 1) == 1
    mixer = jnp.concatenate(
        [
            jnp.where(imaginary, -steer_imag, steer_real),
            jnp.where(imaginary, steer_real, steer_imag),
        ],
        axis=0,
    )
    for i in range(8):
        data = data_ref[pl.ds(i, 2 * PASSES, stride=8), :]
        tomo = jnp.dot(mixer, data, precision=highest, preferred_element_type=F32)
        real, imag = tomo[:HEIGHTS], tomo[HEIGHTS:]
        out_ref[pl.ds(i, HEIGHTS, stride=8), :] = real * real + imag * imag


VMEM = pl.BlockSpec(memory_space=pltpu.VMEM)
SMEM = pl.BlockSpec(memory_space=pltpu.SMEM)


def body(
    echo,
    chirp,
    pair_swap,
    range_shift,
    angle_shift,
    range_taps,
    angle_taps,
    phase_rates,
    invert,
    baseline_index,
):
    tables = (pair_swap, range_shift, angle_shift, range_taps, angle_taps, phase_rates)
    blocks = pl.pallas_call(
        compress_kernel,
        name="compress",
        out_shape=jax.ShapeDtypeStruct((N_AP, 2 * PULSES, LANES), F32),
        in_specs=[VMEM, VMEM] + [SMEM] * 6,
        out_specs=VMEM,
        scratch_shapes=[
            pltpu.VMEM((PULSES, NS // LANES + 5, 2, LANES), F32),
            pltpu.VMEM((2 * PULSES, (TILES + WINDOW // LANES) * LANES), F32),
            pltpu.VMEM((2, TILES * 2 * PULSES, LANES), F32),
            pltpu.VMEM((2, 2, TILES + 1, PULSES, LANES), F32),
        ],
    )(echo, chirp, *tables)
    blocks = lax.all_to_all(blocks, "ap", split_axis=0, concat_axis=0, tiled=True)
    stacks = pl.pallas_call(
        merge_kernel,
        name="merge",
        out_shape=jax.ShapeDtypeStruct((PASSES, 16, LANES), F32),
        in_specs=[VMEM] + [SMEM] * 6,
        out_specs=VMEM,
        scratch_shapes=[
            pltpu.VMEM((2, 2, 2, LANES, LANES), F32),
            pltpu.VMEM((2, 2, RW, LANES), F32),
        ],
    )(blocks, *tables)
    stacks = lax.all_to_all(stacks, "pass", split_axis=0, concat_axis=0, tiled=True)
    power = pl.pallas_call(
        invert_kernel,
        name="invert",
        out_shape=jax.ShapeDtypeStruct((HEIGHTS * 8, LANES), F32),
        in_specs=[VMEM, VMEM, SMEM],
        out_specs=VMEM,
    )(stacks.reshape(PASSES * 16, LANES), invert, baseline_index)
    return power.reshape(1, HEIGHTS, 1, RW * BEAMS // PASSES)


def solution(mesh):
    return jax.shard_map(
        body,
        mesh=mesh,
        in_specs=(
            P("pass", "ap", None, None),
            P(),
            P("pass", None),
            P("pass", None, None),
            P("pass", None, None, None),
            P(),
            P(),
            P(),
            P(),
            P(),
        ),
        out_specs=P("pass", None, "ap", None),
        check_vma=False,
    )
```

```python
import math

import jax
import jax.numpy as jnp
from jax import lax
from jax.experimental import pallas as pl
from jax.experimental.pallas import tpu as pltpu
from jax.sharding import PartitionSpec as P

NR = 2048
TAPS = 1024
NS = 3072
HEIGHTS = 64
KT = 8
ORIGIN = KT // 2 - 1
BASES = 32
LEVELS = 8
LOCAL = 3
CROSS = 5
PULSES = 8
N_AP = 32
PASSES = 16
RW = 64
BEAMS = 256
LANES = 128
TILES = 17
BLOCKS = NR // LANES
FRAME_ROWS = 24
WINDOW = TAPS + LANES
SQRT_HALF = math.sqrt(0.5)
F32 = jnp.float32
BF16 = jnp.bfloat16

ROWS = (96, 88, 80, 72, 64)


def iota(shape, dim):
    return lax.broadcasted_iota(jnp.int32, shape, dim)


def sincos(x):
    turns = jnp.floor(x * (2.0 / math.pi) + 0.5)
    quadrant = turns.astype(jnp.int32)
    y = x - turns * 1.5703125
    y = y - turns * 4.837512969970703e-4
    y = y - turns * 7.54978995489188e-8
    y2 = y * y
    s = y * (1.0 + y2 * (-1.6666654611e-1 + y2 * (8.3321608736e-3 + y2 * -1.9515295891e-4)))
    c = 1.0 - 0.5 * y2 + y2 * y2 * (4.166664568298827e-2 + y2 * (-1.388731625493765e-3 + y2 * 2.443315711809948e-5))
    swap = (quadrant & 1) == 1
    cos_abs = jnp.where(swap, s, c)
    sin_abs = jnp.where(swap, c, s)
    cos = jnp.where(((quadrant + 1) & 2) == 2, -cos_abs, cos_abs)
    sin = jnp.where((quadrant & 2) == 2, -sin_abs, sin_abs)
    return cos, sin


def complex_mul(ar, ai, br, bi):
    return ar * br - ai * bi, ar * bi + ai * br


def reverse_bits(value):
    result = 0
    for digit in range(CROSS):
        result = result + (value // 2**digit % 2) * 2 ** (CROSS - 1 - digit)
    return result


def role(tables, level, child):
    flip = tables[0][0, level]
    return flip if child == 0 else 1 - flip


def step_offset(tables, level, child):
    return tables[1][0, role(tables, level, child), level] - ORIGIN


def slope_and_bend(tables, level, e, parity):
    rates = tables[5]
    slope = jnp.where(parity == 1, rates[e, 1, 0, level], rates[e, 0, 0, level])
    bend = jnp.where(parity == 1, rates[e, 1, 1, level], rates[e, 0, 1, level])
    return slope * (8.0 / NR), 8.0 * bend


def split(value):
    high = value.astype(BF16).astype(F32)
    return high, value - high


def start_copies(sources, targets, arrived):
    copies = [
        pltpu.make_async_copy(source, target, arrived.at[i])
        for i, (source, target) in enumerate(zip(sources, targets))
    ]
    for copy in copies:
        copy.start()
    return copies


def compress_kernel(
    echo_ref,
    chirp_ref,
    swap_ref,
    range_shift_ref,
    angle_shift_ref,
    range_taps_ref,
    angle_taps_ref,
    rates_ref,
    out_ref,
    echo,
    chirp,
    echo_rows,
    product,
    shifting,
    framed,
    images,
    *scalars,
):
    *tables, arrived = scalars
    fetch_chirp = pltpu.make_async_copy(chirp_ref, chirp, arrived.at[len(tables)])
    fetch_chirp.start()
    fetch = pltpu.make_async_copy(echo_ref.at[0], echo, arrived.at[len(tables) + 1])
    fetch.start()
    fetch_tables = start_copies(
        (
            swap_ref,
            range_shift_ref,
            angle_shift_ref,
            range_taps_ref,
            angle_taps_ref,
            rates_ref,
        ),
        tables,
        arrived,
    )
    _, _, angle_shift_ref, range_taps_ref, angle_taps_ref, _ = tables
    rows8 = iota((PULSES, LANES), 0)
    lanes8 = iota((PULSES, LANES), 1)

    fetch_chirp.wait()
    bands = []
    row = iota((LANES, LANES), 0)
    column = iota((LANES, LANES), 1)
    for part in range(2):
        previous = jnp.zeros((LANES, LANES), F32)
        pieces = []
        for t in range(WINDOW // LANES):
            if t * LANES < TAPS:
                samples = chirp[part : part + 1, t * LANES : (t + 1) * LANES].astype(F32)
                current = pltpu.roll(
                    jnp.broadcast_to(samples, (LANES, LANES)), 0, 1, stride=1, stride_axis=0
                )
            else:
                current = jnp.zeros((LANES, LANES), F32)
            pieces.append(jnp.where(column >= row, current, previous).astype(BF16))
            previous = current
        bands.append(jnp.concatenate(pieces, axis=1))
    banded = jnp.concatenate(bands, axis=0)
    for copy in fetch_tables:
        copy.wait()

    position = lax.axis_index("ap")
    offset_above = jnp.int32(0)
    for level in range(LOCAL, LEVELS):
        bit = position // 2 ** (level - LOCAL) % 2
        offset_above = offset_above + jnp.where(
            bit == 1, step_offset(tables, level, 1), step_offset(tables, level, 0)
        )
    local_steps = [
        [step_offset(tables, level, child) for child in range(2)] for level in range(LOCAL)
    ]
    shifting[:, :8] = jnp.zeros((2 * PULSES, 8, LANES), F32)
    shifting[:, 8 + BLOCKS :] = jnp.zeros((2 * PULSES, 16, LANES), F32)

    fetch.wait()
    for n in range(PULSES):
        echo_rows[2 * n : 2 * n + 2, :] = echo[n].astype(F32)
    signal = echo_rows[...].astype(BF16)
    windows = jnp.concatenate(
        [signal[:, b * LANES : b * LANES + WINDOW] for b in range(BLOCKS)], axis=0
    )
    correlated = lax.dot_general(
        windows, banded, (((1,), (1,)), ((), ())), preferred_element_type=F32
    )
    for part in range(2):
        product[part] = correlated[:, part * LANES : (part + 1) * LANES]

    for n in range(PULSES):
        total = offset_above
        for level in range(LOCAL):
            total = total + local_steps[level][n >> level & 1]
        whole = total >> 7
        rest = total & (LANES - 1)
        even, odd = (
            [product[part, pl.ds(2 * n + i, BLOCKS, stride=16), :] for part in range(2)]
            for i in range(2)
        )
        keep = iota((FRAME_ROWS, LANES), 1) < LANES - rest
        for part, value in enumerate((even[0] + odd[1], odd[0] - even[1])):
            i = 2 * n + part
            shifting[i, 8 : 8 + BLOCKS] = pltpu.roll(value, (LANES - rest) & (LANES - 1), 1)
            left = shifting[i, pl.ds(8 + whole, FRAME_ROWS), :]
            right = shifting[i, pl.ds(9 + whole, FRAME_ROWS), :]
            framed[i * FRAME_ROWS : (i + 1) * FRAME_ROWS] = jnp.where(keep, left, right)

    def load(level, part, b):
        if level == 0:
            return framed[pl.ds(part * FRAME_ROWS + b, PULSES, stride=2 * FRAME_ROWS), :]
        return images[level % 2, part, b]

    for level in range(LOCAL):
        beams = 2**level
        roles = [role(tables, level, child) for child in range(2)]
        in_child = rows8 >> level & 1
        tap_rows = [
            jnp.where(
                in_child == 1,
                range_taps_ref[level, roles[1], u],
                range_taps_ref[level, roles[0], u],
            )
            for u in range(KT)
        ]

        row16 = iota((2 * PULSES, LANES), 0)
        lane16 = iota((2 * PULSES, LANES), 1)
        of_child = row16 >> 3
        row_out = row16 & 7
        parity16 = row16 & 1

        def of_row(pick):
            return jnp.where(
                of_child == 1,
                jnp.where(parity16 == 1, pick(roles[1], 1), pick(roles[1], 0)),
                jnp.where(parity16 == 1, pick(roles[0], 1), pick(roles[0], 0)),
            )

        shift = of_row(lambda e, h: angle_shift_ref[0, e, h, level])
        beam = row_out % (2 * beams) // 2
        first = (row_out // (2 * beams) * 2 + of_child) * beams
        weights = jnp.zeros((2 * PULSES, LANES), F32)
        for u in range(KT):
            picked = first + jnp.clip(beam + (u - ORIGIN) + shift, 0, beams - 1)
            tap = of_row(lambda e, h: angle_taps_ref[level, e, h, u])
            weights = weights + jnp.where((lane16 & 7) == picked, tap, 0.0)
        high, low = split(weights)
        piece = lane16 >> 3
        left_side = jnp.where(piece < 2, high, jnp.where(piece == 2, low, 0.0)).astype(BF16)[:, :32]

        offset_out = jnp.full((PULSES, LANES), offset_above, jnp.int32)
        for later in range(level + 1, LOCAL):
            offset_out = offset_out + jnp.where(
                (rows8 >> later & 1) == 1, local_steps[later][1], local_steps[later][0]
            )
        cell_out = offset_out + lanes8
        beam_fraction = (rows8 % (2 * beams)).astype(F32) / (2.0 * beams)
        waves = []
        steps = []
        for child in range(2):
            slope, bend = slope_and_bend(tables, level, roles[child], rows8 & 1)
            cos, sin = sincos(slope * cell_out.astype(F32) + bend * beam_fraction)
            waves.append((cos * SQRT_HALF, sin * SQRT_HALF))
            steps.append(sincos(slope * float(LANES)))

        def rolls(b):
            found = []
            for part in range(2):
                value = load(level, part, b)
                found.append([value] + [pltpu.roll(value, LANES - u, 1) for u in range(1, KT)])
            return found

        here = rolls(0)
        for b in range(TILES):
            there = rolls(b + 1) if b + 1 < TILES else here
            pieces = []
            for part in range(2):
                total = tap_rows[0] * here[part][0]
                for u in range(1, KT):
                    moved = jnp.where(lanes8 < LANES - u, here[part][u], there[part][u])
                    total = total + tap_rows[u] * moved
                high, low = split(total)
                pieces.append(
                    jnp.concatenate([high, low, high, jnp.zeros((PULSES, LANES), F32)], axis=0)
                )
            right_side = jnp.concatenate(pieces, axis=1).astype(BF16)
            steered = jnp.dot(left_side, right_side, preferred_element_type=F32)
            out_real = jnp.zeros((PULSES, LANES), F32)
            out_imag = jnp.zeros((PULSES, LANES), F32)
            for child in range(2):
                rows = steered[child * PULSES : (child + 1) * PULSES]
                real, imag = complex_mul(*waves[child], rows[:, :LANES], rows[:, LANES:])
                out_real = out_real + real
                out_imag = out_imag + imag
                waves[child] = complex_mul(*waves[child], *steps[child])
            where_r = cell_out + b * LANES
            inside = (where_r >= 0) & (where_r < NR)
            images[(level + 1) % 2, 0, b] = jnp.where(inside, out_real, 0.0)
            images[(level + 1) % 2, 1, b] = jnp.where(inside, out_imag, 0.0)
            here = there

    last = LOCAL % 2
    for block in range(N_AP):
        start = reverse_bits(block) * RW
        t = start // LANES
        for part in range(2):
            if start % LANES == 0:
                value = images[last, part, t]
            else:
                value = jnp.where(
                    lanes8 < RW,
                    pltpu.roll(images[last, part, t], RW, 1),
                    pltpu.roll(images[last, part, t + 1], RW, 1),
                )
            out_ref[block, part * PULSES : (part + 1) * PULSES, :] = value


def column_offset(tables, level, column):
    offset = jnp.zeros_like(column)
    for later in range(level + 1, LEVELS):
        bit = column >> (7 - (later - level - 1)) & 1
        offset = offset + jnp.where(
            bit == 1, step_offset(tables, later, 1), step_offset(tables, later, 0)
        )
    return offset


def tables_kernel(
    swap_ref,
    range_shift_ref,
    angle_shift_ref,
    range_taps_ref,
    angle_taps_ref,
    rates_ref,
    invert_ref,
    baseline_ref,
    weights_ref,
    waves_ref,
    taps_ref,
    mixer_ref,
    invert,
    baseline,
    *scalars,
):
    *tables, arrived = scalars
    for copy in start_copies(
        (
            swap_ref,
            range_shift_ref,
            angle_shift_ref,
            range_taps_ref,
            angle_taps_ref,
            rates_ref,
            invert_ref,
            baseline_ref,
        ),
        (*tables, invert, baseline),
        arrived,
    ):
        copy.wait()
    _, _, angle_shift_ref, range_taps_ref, angle_taps_ref, _ = tables
    position = lax.axis_index("ap")
    base = reverse_bits(position) * RW
    column = iota((1, 2 * LANES), 1)
    row = iota((LANES, 2 * LANES), 0)
    parity = column & 1
    for k in range(CROSS):
        level = LOCAL + k
        beams = 2**level
        beam = column % (2 * beams) // 2
        first_row = column // (2 * beams) * beams
        beam_fraction = (column % (2 * beams)).astype(F32) / (2.0 * beams)
        cell = iota((8, 2 * LANES), 0) + (base + column_offset(tables, level, column))
        for child in range(2):
            e = role(tables, level, child)
            shift = jnp.where(
                parity == 1, angle_shift_ref[0, e, 1, level], angle_shift_ref[0, e, 0, level]
            )
            weights = jnp.zeros((LANES, 2 * LANES), F32)
            for u in range(KT):
                tap = jnp.where(
                    parity == 1, angle_taps_ref[level, e, 1, u], angle_taps_ref[level, e, 0, u]
                )
                picked = first_row + jnp.clip(beam + (u - ORIGIN) + shift, 0, beams - 1)
                weights = weights + jnp.where(row == picked, tap, 0.0)
            high, low = split(weights)
            at = 2 * k + child
            weights_ref[at, :LANES] = high.astype(BF16)
            weights_ref[at, LANES:] = low.astype(BF16)
            slope, bend = slope_and_bend(tables, level, e, parity)
            cos, sin = sincos(slope * cell.astype(F32) + bend * beam_fraction)
            waves_ref[at, 0] = cos * SQRT_HALF
            waves_ref[at, 1] = sin * SQRT_HALF
            cos, sin = sincos(jnp.broadcast_to(slope * 8.0, (8, 2 * LANES)))
            waves_ref[at, 2] = cos
            waves_ref[at, 3] = sin
            waves_ref[at, 4] = cell.astype(F32)
            for u in range(KT):
                taps_ref[at, u] = jnp.full((8, LANES), range_taps_ref[level, e, u], F32)

    lane = iota((1, LANES), 1)
    wanted = jnp.zeros((1, LANES), jnp.int32)
    for p in range(PASSES):
        wanted = jnp.where(lane % (2 * PASSES) // 2 == p, baseline[p], wanted)
    chosen = (iota((BASES, LANES), 0) == wanted).astype(F32)
    steer = [
        lax.dot_general(
            invert[part],
            chosen,
            (((0,), (0,)), ((), ())),
            precision=lax.Precision.HIGHEST,
            preferred_element_type=F32,
        )
        for part in range(2)
    ]
    imaginary = (lane & 1) == 1
    high, low = split(
        jnp.concatenate(
            [jnp.where(imaginary, -steer[1], steer[0]), jnp.where(imaginary, steer[0], steer[1])],
            axis=0,
        )
    )
    piece = lane // (2 * PASSES)
    mixer_ref[...] = jnp.where(piece < 2, high, jnp.where(piece == 2, low, 0.0)).astype(BF16)


def merge_kernel(
    blocks_ref,
    weights_ref,
    waves_ref,
    taps_ref,
    out_ref,
    blocks,
    weights,
    waves,
    taps,
    images,
    final,
    arrived,
):
    fetches = [pltpu.make_async_copy(blocks_ref, blocks, arrived.at[CROSS])]
    fetches += [
        pltpu.make_async_copy(
            weights_ref.at[pl.ds(2 * k, 2)], weights.at[pl.ds(2 * k, 2)], arrived.at[k]
        )
        for k in range(CROSS)
    ]
    fetches.append(pltpu.make_async_copy(waves_ref, waves, arrived.at[CROSS + 1]))
    fetches.append(pltpu.make_async_copy(taps_ref, taps, arrived.at[CROSS + 2]))
    for fetch in fetches:
        fetch.start()
    fetches[0].wait()
    for child in range(2):
        order = []
        for i in range(N_AP // 2):
            order.append(
                child + 2 * (i >> 3 & 1) + 4 * (i >> 2 & 1) + 8 * (i >> 1 & 1) + 16 * (i & 1)
            )
        for part in range(2):
            stacked = jnp.concatenate(
                [blocks[g, part * PULSES : (part + 1) * PULSES, :] for g in order], axis=0
            )
            images[0, child, part] = stacked.T

    fetches[CROSS + 1].wait()
    fetches[CROSS + 2].wait()
    for k in range(CROSS):
        rows = ROWS[k]
        source, target = k % 2, 1 - k % 2
        last = k == CROSS - 1
        fetches[1 + k].wait()
        steered = []
        for child in range(2):
            tap = [
                jnp.concatenate([taps[2 * k + child, u]] * (rows // 8), axis=0) for u in range(KT)
            ]
            parts = []
            for part in range(2):
                total = tap[0] * images[source, child, part, 0:rows, :]
                for u in range(1, KT):
                    total = total + tap[u] * images[source, child, part, u : u + rows, :]
                parts.append(total)
            ranged = jnp.concatenate(parts, axis=0)
            high = ranged.astype(BF16)
            low = (ranged - high.astype(F32)).astype(BF16)
            matrix = weights[2 * k + child]
            steered.append(
                jnp.dot(
                    jnp.concatenate([high, low, high], axis=1),
                    jnp.concatenate([matrix[:LANES], matrix[:LANES], matrix[LANES:]], axis=0),
                    preferred_element_type=F32,
                )
            )
        turning = [(waves[2 * k + child, 0], waves[2 * k + child, 1]) for child in range(2)]
        steps = [(waves[2 * k + child, 2], waves[2 * k + child, 3]) for child in range(2)]
        for m in range(rows // 8):
            out_real = jnp.zeros((8, 2 * LANES), F32)
            out_imag = jnp.zeros((8, 2 * LANES), F32)
            for child in range(2):
                real, imag = complex_mul(
                    *turning[child],
                    steered[child][8 * m : 8 * m + 8],
                    steered[child][rows + 8 * m : rows + 8 * m + 8],
                )
                out_real = out_real + real
                out_imag = out_imag + imag
                turning[child] = complex_mul(*turning[child], *steps[child])
            if not last:
                where_r = waves[2 * k, 4] + float(8 * m)
                inside = (where_r >= 0) & (where_r < NR)
                out_real = jnp.where(inside, out_real, 0.0)
                out_imag = jnp.where(inside, out_imag, 0.0)
            for part, value in enumerate((out_real, out_imag)):
                for side in range(2):
                    piece = value[:, side * LANES : (side + 1) * LANES]
                    if last:
                        final[part, side, 8 * m : 8 * m + 8] = piece
                    else:
                        images[target, side, part, 8 * m : 8 * m + 8, :] = piece

    block_of = iota((8, LANES), 1) // 16
    for part in range(2):
        for side in range(2):
            values = [final[part, side, pl.ds(i, 8, stride=8), :] for i in range(8)]
            for d in (4, 2, 1):
                clear = (block_of & d) == 0
                for i in range(8):
                    if i & d == 0:
                        a, b = values[i], values[i | d]
                        values[i] = jnp.where(clear, a, pltpu.roll(b, 16 * d, 1))
                        values[i | d] = jnp.where(clear, pltpu.roll(a, LANES - 16 * d, 1), b)
            for q in range(8):
                out_ref[side * 8 + q, part * 8 : part * 8 + 8, :] = values[q]


def invert_kernel(data_ref, mixer_ref, out_ref, data, arrived):
    fetch = pltpu.make_async_copy(data_ref, data, arrived)
    fetch.start()
    mixer = mixer_ref[...]
    fetch.wait()
    for i in range(8):
        high, low = split(data[pl.ds(i, 2 * PASSES, stride=8), :])
        right_side = jnp.concatenate([high, low, high, jnp.zeros_like(high)], axis=0)
        tomo = jnp.dot(mixer, right_side.astype(BF16), preferred_element_type=F32)
        real, imag = tomo[:HEIGHTS], tomo[HEIGHTS:]
        out_ref[pl.ds(i, HEIGHTS, stride=8), :] = real * real + imag * imag


VMEM = pl.BlockSpec(memory_space=pltpu.VMEM)
ANY = pl.BlockSpec(memory_space=pl.ANY)
HBM = pl.BlockSpec(memory_space=pltpu.HBM)
LIMIT = 16 << 20


def in_hbm(array):
    return pltpu.with_memory_space_constraint(array, pltpu.HBM)


def body(
    echo,
    chirp,
    pair_swap,
    range_shift,
    angle_shift,
    range_taps,
    angle_taps,
    phase_rates,
    invert,
    baseline_index,
):
    tables = (
        pair_swap,
        jnp.transpose(range_shift, (0, 2, 1)),
        jnp.transpose(angle_shift, (0, 2, 3, 1)),
        range_taps,
        angle_taps,
        jnp.transpose(phase_rates, (1, 2, 3, 0)),
    )
    tables = [in_hbm(table) for table in tables]
    held = [pltpu.SMEM(table.shape, table.dtype) for table in tables]
    params = pltpu.CompilerParams(vmem_limit_bytes=LIMIT)
    blocks = pl.pallas_call(
        compress_kernel,
        name="compress",
        out_shape=jax.ShapeDtypeStruct((N_AP, 2 * PULSES, LANES), F32),
        in_specs=[HBM] * 8,
        out_specs=VMEM,
        scratch_shapes=[
            pltpu.VMEM((PULSES, 2, NS), BF16),
            pltpu.VMEM((2, TAPS), BF16),
            pltpu.VMEM((2 * PULSES, NS), F32),
            pltpu.VMEM((2, 2 * PULSES * BLOCKS, LANES), F32),
            pltpu.VMEM((2 * PULSES, 24 + BLOCKS, LANES), F32),
            pltpu.VMEM((2 * PULSES * FRAME_ROWS, LANES), F32),
            pltpu.VMEM((2, 2, TILES, PULSES, LANES), F32),
            *held,
            pltpu.SemaphoreType.DMA((8,)),
        ],
        compiler_params=params,
        cost_estimate=pl.CostEstimate(flops=10**8, bytes_accessed=10**6, transcendentals=0),
    )(in_hbm(echo), in_hbm(chirp), *tables)
    weights, waves, taps, mixer = pl.pallas_call(
        tables_kernel,
        name="tables",
        out_shape=(
            jax.ShapeDtypeStruct((2 * CROSS, 2 * LANES, 2 * LANES), BF16),
            jax.ShapeDtypeStruct((2 * CROSS, 5, 8, 2 * LANES), F32),
            jax.ShapeDtypeStruct((2 * CROSS, KT, 8, LANES), F32),
            jax.ShapeDtypeStruct((2 * HEIGHTS, LANES), BF16),
        ),
        in_specs=[HBM] * 8,
        out_specs=(VMEM,) * 4,
        scratch_shapes=[
            pltpu.VMEM((2, BASES, HEIGHTS), F32),
            pltpu.SMEM((PASSES,), jnp.int32),
            *held,
            pltpu.SemaphoreType.DMA((8,)),
        ],
        compiler_params=params,
        cost_estimate=pl.CostEstimate(flops=10**8, bytes_accessed=10**6, transcendentals=0),
    )(*tables, in_hbm(jnp.transpose(invert, (0, 2, 1))), in_hbm(baseline_index))
    blocks = lax.all_to_all(blocks, "ap", split_axis=0, concat_axis=0, tiled=True)
    stacks = pl.pallas_call(
        merge_kernel,
        name="merge",
        out_shape=jax.ShapeDtypeStruct((PASSES, 16, LANES), F32),
        in_specs=[ANY] * 4,
        out_specs=VMEM,
        scratch_shapes=[
            pltpu.VMEM((N_AP, 2 * PULSES, LANES), F32),
            pltpu.VMEM((2 * CROSS, 2 * LANES, 2 * LANES), BF16),
            pltpu.VMEM((2 * CROSS, 5, 8, 2 * LANES), F32),
            pltpu.VMEM((2 * CROSS, KT, 8, LANES), F32),
            pltpu.VMEM((2, 2, 2, LANES, LANES), F32),
            pltpu.VMEM((2, 2, RW, LANES), F32),
            pltpu.SemaphoreType.DMA((CROSS + 3,)),
        ],
        compiler_params=params,
        cost_estimate=pl.CostEstimate(flops=10**8, bytes_accessed=10**6, transcendentals=0),
    )(blocks, weights, waves, taps)
    stacks = lax.all_to_all(stacks, "pass", split_axis=0, concat_axis=0, tiled=True)
    power = pl.pallas_call(
        invert_kernel,
        name="invert",
        out_shape=jax.ShapeDtypeStruct((HEIGHTS * 8, LANES), F32),
        in_specs=[ANY, VMEM],
        out_specs=VMEM,
        scratch_shapes=[pltpu.VMEM((PASSES * 16, LANES), F32), pltpu.SemaphoreType.DMA],
        compiler_params=params,
        cost_estimate=pl.CostEstimate(flops=10**8, bytes_accessed=10**6, transcendentals=0),
    )(stacks.reshape(PASSES * 16, LANES), mixer)
    return power.reshape(1, HEIGHTS, 1, RW * BEAMS // PASSES)


def solution(mesh):
    return jax.shard_map(
        body,
        mesh=mesh,
        in_specs=(
            P("pass", "ap", None, None),
            P(),
            P("pass", None),
            P("pass", None, None),
            P("pass", None, None, None),
            P(),
            P(),
            P(),
            P(),
            P(),
        ),
        out_specs=P("pass", None, "ap", None),
        check_vma=False,
    )
```

```python
import math

import jax
import jax.numpy as jnp
from jax import lax
from jax.experimental import pallas as pl
from jax.experimental.pallas import tpu as pltpu
from jax.sharding import PartitionSpec as P

NR = 2048
TAPS = 1024
NS = 3072
HEIGHTS = 64
KT = 8
ORIGIN = KT // 2 - 1
RMAX = 16
BASES = 32
LEVELS = 8
LOCAL = 3
CROSS = 5
PULSES = 8
N_AP = 32
PASSES = 16
RW = 64
QUARTERS = 4
BEAMS = 256
LANES = 128
TILES = 17
BLOCKS = NR // LANES
FRAME_ROWS = 24
WINDOW = TAPS + LANES
SQRT_HALF = math.sqrt(0.5)
F32 = jnp.float32
BF16 = jnp.bfloat16

ROWS = (96, 88, 80, 72, 64)


def iota(shape, dim):
    return lax.broadcasted_iota(jnp.int32, shape, dim)


def sincos(x):
    turns = jnp.floor(x * (2.0 / math.pi) + 0.5)
    quadrant = turns.astype(jnp.int32)
    y = x - turns * 1.5703125
    y = y - turns * 4.837512969970703e-4
    y = y - turns * 7.54978995489188e-8
    y2 = y * y
    s = y * (1.0 + y2 * (-1.6666654611e-1 + y2 * (8.3321608736e-3 + y2 * -1.9515295891e-4)))
    c = 1.0 - 0.5 * y2 + y2 * y2 * (4.166664568298827e-2 + y2 * (-1.388731625493765e-3 + y2 * 2.443315711809948e-5))
    swap = (quadrant & 1) == 1
    cos_abs = jnp.where(swap, s, c)
    sin_abs = jnp.where(swap, c, s)
    cos = jnp.where(((quadrant + 1) & 2) == 2, -cos_abs, cos_abs)
    sin = jnp.where((quadrant & 2) == 2, -sin_abs, sin_abs)
    return cos, sin


def complex_mul(ar, ai, br, bi):
    return ar * br - ai * bi, ar * bi + ai * br


def reverse_bits(value):
    result = 0
    for digit in range(CROSS):
        result = result + (value // 2**digit % 2) * 2 ** (CROSS - 1 - digit)
    return result


def role(tables, level, child):
    flip = tables[0][0, level]
    return flip if child == 0 else 1 - flip


def step_offset(tables, level, child):
    return tables[1][0, role(tables, level, child), level] - ORIGIN


def slope_and_bend(tables, level, e, parity):
    rates = tables[5]
    slope = jnp.where(parity == 1, rates[e, 1, 0, level], rates[e, 0, 0, level])
    bend = jnp.where(parity == 1, rates[e, 1, 1, level], rates[e, 0, 1, level])
    return slope * (8.0 / NR), 8.0 * bend


def split(value):
    high = value.astype(BF16).astype(F32)
    return high, value - high


def start_copies(sources, targets, arrived):
    copies = [
        pltpu.make_async_copy(source, target, arrived.at[i])
        for i, (source, target) in enumerate(zip(sources, targets))
    ]
    for copy in copies:
        copy.start()
    return copies


def compress_kernel(
    echo_ref,
    chirp_ref,
    swap_ref,
    range_shift_ref,
    angle_shift_ref,
    range_taps_ref,
    angle_taps_ref,
    rates_ref,
    out_ref,
    echo,
    chirp,
    echo_rows,
    product,
    shifting,
    framed,
    images,
    outgoing,
    *scalars,
):
    *tables, arrived = scalars
    fetch_chirp = pltpu.make_async_copy(chirp_ref, chirp, arrived.at[len(tables)])
    fetch_chirp.start()
    fetch = pltpu.make_async_copy(echo_ref.at[0], echo, arrived.at[len(tables) + 1])
    fetch.start()
    fetch_tables = start_copies(
        (
            swap_ref,
            range_shift_ref,
            angle_shift_ref,
            range_taps_ref,
            angle_taps_ref,
            rates_ref,
        ),
        tables,
        arrived,
    )
    _, _, angle_shift_ref, range_taps_ref, angle_taps_ref, _ = tables
    rows8 = iota((PULSES, LANES), 0)
    lanes8 = iota((PULSES, LANES), 1)

    fetch_chirp.wait()
    bands = []
    row = iota((LANES, LANES), 0)
    column = iota((LANES, LANES), 1)
    for part in range(2):
        previous = jnp.zeros((LANES, LANES), F32)
        pieces = []
        for t in range(WINDOW // LANES):
            if t * LANES < TAPS:
                samples = chirp[part : part + 1, t * LANES : (t + 1) * LANES].astype(F32)
                current = pltpu.roll(
                    jnp.broadcast_to(samples, (LANES, LANES)), 0, 1, stride=1, stride_axis=0
                )
            else:
                current = jnp.zeros((LANES, LANES), F32)
            pieces.append(jnp.where(column >= row, current, previous).astype(BF16))
            previous = current
        bands.append(jnp.concatenate(pieces, axis=1))
    banded = jnp.concatenate(bands, axis=0)

    shifting[:, :8] = jnp.zeros((2 * PULSES, 8, LANES), F32)
    shifting[:, 8 + BLOCKS :] = jnp.zeros((2 * PULSES, 16, LANES), F32)

    fetch.wait()
    for n in range(PULSES):
        echo_rows[2 * n : 2 * n + 2, :] = echo[n].astype(F32)
    signal = echo_rows[...].astype(BF16)
    windows = jnp.concatenate(
        [signal[:, b * LANES : b * LANES + WINDOW] for b in range(BLOCKS)], axis=0
    )
    correlated = lax.dot_general(
        windows, banded, (((1,), (1,)), ((), ())), preferred_element_type=F32
    )
    for part in range(2):
        product[part] = correlated[:, part * LANES : (part + 1) * LANES]

    for copy in fetch_tables:
        copy.wait()

    position = lax.axis_index("ap")
    offset_above = jnp.int32(0)
    for level in range(LOCAL, LEVELS):
        bit = position // 2 ** (level - LOCAL) % 2
        offset_above = offset_above + jnp.where(
            bit == 1, step_offset(tables, level, 1), step_offset(tables, level, 0)
        )
    local_steps = [
        [step_offset(tables, level, child) for child in range(2)] for level in range(LOCAL)
    ]

    def prepare(level):
        beams = 2**level
        roles = [role(tables, level, child) for child in range(2)]
        in_child = rows8 >> level & 1
        tap_rows = [
            jnp.where(
                in_child == 1,
                range_taps_ref[level, roles[1], u],
                range_taps_ref[level, roles[0], u],
            )
            for u in range(KT)
        ]

        row16 = iota((2 * PULSES, LANES), 0)
        lane16 = iota((2 * PULSES, LANES), 1)
        of_child = row16 >> 3
        row_out = row16 & 7
        parity16 = row16 & 1

        def of_row(pick):
            return jnp.where(
                of_child == 1,
                jnp.where(parity16 == 1, pick(roles[1], 1), pick(roles[1], 0)),
                jnp.where(parity16 == 1, pick(roles[0], 1), pick(roles[0], 0)),
            )

        shift = of_row(lambda e, h: angle_shift_ref[0, e, h, level])
        beam = row_out % (2 * beams) // 2
        first = (row_out // (2 * beams) * 2 + of_child) * beams
        weights = jnp.zeros((2 * PULSES, LANES), F32)
        for u in range(KT):
            picked = first + jnp.clip(beam + (u - ORIGIN) + shift, 0, beams - 1)
            tap = of_row(lambda e, h: angle_taps_ref[level, e, h, u])
            weights = weights + jnp.where((lane16 & 7) == picked, tap, 0.0)
        high, low = split(weights)
        piece = lane16 >> 3
        left_side = jnp.where(piece < 2, high, jnp.where(piece == 2, low, 0.0)).astype(BF16)[:, :32]

        offset_out = jnp.full((PULSES, LANES), offset_above, jnp.int32)
        for later in range(level + 1, LOCAL):
            offset_out = offset_out + jnp.where(
                (rows8 >> later & 1) == 1, local_steps[later][1], local_steps[later][0]
            )
        cell_out = offset_out + lanes8
        beam_fraction = (rows8 % (2 * beams)).astype(F32) / (2.0 * beams)
        waves = []
        steps = []
        for child in range(2):
            slope, bend = slope_and_bend(tables, level, roles[child], rows8 & 1)
            cos, sin = sincos(slope * cell_out.astype(F32) + bend * beam_fraction)
            waves.append((cos * SQRT_HALF, sin * SQRT_HALF))
            steps.append(sincos(slope * float(LANES)))

        return tap_rows, left_side, cell_out, waves, steps

    totals = []
    for n in range(PULSES):
        total = offset_above
        for level in range(LOCAL):
            total = total + local_steps[level][n >> level & 1]
        totals.append(total)
        rest = total & (LANES - 1)
        even, odd = (
            [product[part, pl.ds(2 * n + i, BLOCKS, stride=16), :] for part in range(2)]
            for i in range(2)
        )
        for part, value in enumerate((even[0] + odd[1], odd[0] - even[1])):
            shifting[2 * n + part, 8 : 8 + BLOCKS] = pltpu.roll(
                value, (LANES - rest) & (LANES - 1), 1
            )
    lane = iota((FRAME_ROWS, LANES), 1)
    for n in range(PULSES):
        whole = totals[n] >> 7
        keep = lane < LANES - (totals[n] & (LANES - 1))
        for part in range(2):
            i = 2 * n + part
            left = shifting[i, pl.ds(8 + whole, FRAME_ROWS), :]
            right = shifting[i, pl.ds(9 + whole, FRAME_ROWS), :]
            framed[i * FRAME_ROWS : (i + 1) * FRAME_ROWS] = jnp.where(keep, left, right)

    sends = []

    def send(window, values):
        block = reverse_bits(window)
        for part in range(2):
            outgoing[block % QUARTERS, block // QUARTERS, part * 8 : part * 8 + 8] = values[part]
        if (window + 1) % (N_AP // QUARTERS) == 0:
            quarter = block % QUARTERS
            sends.append(
                pltpu.make_async_copy(
                    outgoing.at[quarter], out_ref.at[:, quarter], arrived.at[8 + quarter]
                )
            )
            sends[-1].start()

    def load(level, part, b):
        if level == 0:
            return framed[pl.ds(part * FRAME_ROWS + b, PULSES, stride=2 * FRAME_ROWS), :]
        return images[level % 2, part, b]

    for level in range(LOCAL):
        tap_rows, left_side, cell_out, waves, steps = prepare(level)

        def turn(value, cells):
            return pltpu.roll(value, LANES - cells, 1)

        def moved(here, there, cells):
            return jnp.where(lanes8 < LANES - cells, here, there)

        def rolls(b):
            values = [load(level, part, b) for part in range(2)]
            return [[value] + [turn(value, u) for u in (1, 2, 3)] for value in values]

        def runs(here, there):
            found = []
            for part in range(2):
                value = here[part][0]
                near, far = tap_rows[0] * value, tap_rows[4] * value
                for u in (1, 2, 3):
                    value = moved(here[part][u], there[part][u], u)
                    near = near + tap_rows[u] * value
                    far = far + tap_rows[4 + u] * value
                found.append((near, turn(far, 4)))
            return found

        here = rolls(0)
        there = rolls(1)
        sums = runs(here, there)
        for b in range(TILES):
            if b + 1 < TILES:
                here, there = there, rolls(b + 2) if b + 2 < TILES else there
                sums_there = runs(here, there)
            pieces = []
            for part in range(2):
                total = sums[part][0] + moved(sums[part][1], sums_there[part][1], 4)
                high, low = split(total)
                pieces.append(
                    jnp.concatenate([high, low, high, jnp.zeros((PULSES, LANES), F32)], axis=0)
                )
            sums = sums_there
            right_side = jnp.concatenate(pieces, axis=1).astype(BF16)
            steered = jnp.dot(left_side, right_side, preferred_element_type=F32)
            terms = []
            for child in range(2):
                rows = steered[child * PULSES : (child + 1) * PULSES]
                terms.append(complex_mul(*waves[child], rows[:, :LANES], rows[:, LANES:]))
                waves[child] = complex_mul(*waves[child], *steps[child])
            values = [a + c for a, c in zip(*terms)]
            if b * LANES < LEVELS * (RMAX + ORIGIN) or (b + 1) * LANES > NR - LEVELS * RMAX:
                where_r = cell_out + b * LANES
                inside = (where_r >= 0) & (where_r < NR)
                values = [jnp.where(inside, value, 0.0) for value in values]
            if level + 1 < LOCAL:
                for part in range(2):
                    images[(level + 1) % 2, part, b] = values[part]
            else:
                turned = [pltpu.roll(value, RW, 1) for value in values]
                if b > 0:
                    joined = [jnp.where(lanes8 < RW, a, c) for a, c in zip(before, turned)]
                    send(2 * b - 1, joined)
                if b < BLOCKS:
                    send(2 * b, values)
                before = turned
    for copy in sends:
        copy.wait()


def column_offset(tables, level, column):
    offset = jnp.zeros_like(column)
    for later in range(level + 1, LEVELS):
        bit = column >> (7 - (later - level - 1)) & 1
        offset = offset + jnp.where(
            bit == 1, step_offset(tables, later, 1), step_offset(tables, later, 0)
        )
    return offset


def tables_kernel(
    swap_ref,
    range_shift_ref,
    angle_shift_ref,
    range_taps_ref,
    angle_taps_ref,
    rates_ref,
    invert_ref,
    baseline_ref,
    weights_ref,
    waves_ref,
    taps_ref,
    mixer_ref,
    invert,
    baseline,
    *scalars,
):
    *tables, arrived = scalars
    for copy in start_copies(
        (
            swap_ref,
            range_shift_ref,
            angle_shift_ref,
            range_taps_ref,
            angle_taps_ref,
            rates_ref,
            invert_ref,
            baseline_ref,
        ),
        (*tables, invert, baseline),
        arrived,
    ):
        copy.wait()
    _, _, angle_shift_ref, range_taps_ref, angle_taps_ref, _ = tables
    position = lax.axis_index("ap")
    base = reverse_bits(position) * RW
    column = iota((1, 2 * LANES), 1)
    row = iota((LANES, 2 * LANES), 0)
    parity = column & 1
    for k in range(CROSS):
        level = LOCAL + k
        beams = 2**level
        beam = column % (2 * beams) // 2
        first_row = column // (2 * beams) * beams
        beam_fraction = (column % (2 * beams)).astype(F32) / (2.0 * beams)
        cell = iota((8, 2 * LANES), 0) + (base + column_offset(tables, level, column))
        for child in range(2):
            e = role(tables, level, child)
            shift = jnp.where(
                parity == 1, angle_shift_ref[0, e, 1, level], angle_shift_ref[0, e, 0, level]
            )
            weights = jnp.zeros((LANES, 2 * LANES), F32)
            for u in range(KT):
                tap = jnp.where(
                    parity == 1, angle_taps_ref[level, e, 1, u], angle_taps_ref[level, e, 0, u]
                )
                picked = first_row + jnp.clip(beam + (u - ORIGIN) + shift, 0, beams - 1)
                weights = weights + jnp.where(row == picked, tap, 0.0)
            high, low = split(weights)
            at = 2 * k + child
            weights_ref[at, :LANES] = high.astype(BF16)
            weights_ref[at, LANES:] = low.astype(BF16)
            slope, bend = slope_and_bend(tables, level, e, parity)
            cos, sin = sincos(slope * cell.astype(F32) + bend * beam_fraction)
            waves_ref[at, 0] = cos * SQRT_HALF
            waves_ref[at, 1] = sin * SQRT_HALF
            cos, sin = sincos(jnp.broadcast_to(slope * 8.0, (8, 2 * LANES)))
            waves_ref[at, 2] = cos
            waves_ref[at, 3] = sin
            waves_ref[at, 4] = cell.astype(F32) - (NR - 1) / 2
            for u in range(KT):
                taps_ref[at, u] = jnp.full((8, LANES), range_taps_ref[level, e, u], F32)

    lane = iota((1, LANES), 1)
    wanted = jnp.zeros((1, LANES), jnp.int32)
    for p in range(PASSES):
        wanted = jnp.where(lane % (2 * PASSES) // 2 == p, baseline[p], wanted)
    chosen = (iota((BASES, LANES), 0) == wanted).astype(F32)
    steer = [
        lax.dot_general(
            invert[part],
            chosen,
            (((0,), (0,)), ((), ())),
            precision=lax.Precision.HIGHEST,
            preferred_element_type=F32,
        )
        for part in range(2)
    ]
    imaginary = (lane & 1) == 1
    high, low = split(
        jnp.concatenate(
            [jnp.where(imaginary, -steer[1], steer[0]), jnp.where(imaginary, steer[0], steer[1])],
            axis=0,
        )
    )
    piece = lane // (2 * PASSES)
    mixer_ref[...] = jnp.where(piece < 2, high, jnp.where(piece == 2, low, 0.0)).astype(BF16)


def merge_kernel(
    blocks,
    weights,
    waves,
    taps,
    out_ref,
    images,
    final,
):
    for child in range(2):
        order = []
        for i in range(N_AP // 2):
            order.append(
                child + 2 * (i >> 3 & 1) + 4 * (i >> 2 & 1) + 8 * (i >> 1 & 1) + 16 * (i & 1)
            )
        for part in range(2):
            stacked = jnp.concatenate(
                [blocks[g, part * PULSES : (part + 1) * PULSES, :] for g in order], axis=0
            )
            images[0, child, part] = stacked.T

    for k in range(CROSS):
        rows = ROWS[k]
        source, target = k % 2, 1 - k % 2
        last = k == CROSS - 1
        steered = []
        for child in range(2):
            tap = [
                jnp.concatenate([taps[2 * k + child, u]] * (rows // 8), axis=0) for u in range(KT)
            ]
            parts = []
            for part in range(2):
                total = tap[0] * images[source, child, part, 0:rows, :]
                for u in range(1, KT):
                    total = total + tap[u] * images[source, child, part, u : u + rows, :]
                parts.append(total)
            ranged = jnp.concatenate(parts, axis=0)
            high = ranged.astype(BF16)
            low = (ranged - high.astype(F32)).astype(BF16)
            matrix = weights[2 * k + child]
            steered.append(
                jnp.dot(
                    jnp.concatenate([high, low, high], axis=1),
                    jnp.concatenate([matrix[:LANES], matrix[:LANES], matrix[LANES:]], axis=0),
                    preferred_element_type=F32,
                )
            )
        turning = [(waves[2 * k + child, 0], waves[2 * k + child, 1]) for child in range(2)]
        steps = [(waves[2 * k + child, 2], waves[2 * k + child, 3]) for child in range(2)]
        for m in range(rows // 8):
            terms = []
            for child in range(2):
                terms.append(
                    complex_mul(
                        *turning[child],
                        steered[child][8 * m : 8 * m + 8],
                        steered[child][rows + 8 * m : rows + 8 * m + 8],
                    )
                )
                turning[child] = complex_mul(*turning[child], *steps[child])
            values = [a + c for a, c in zip(*terms)]
            if not last:
                inside = jnp.abs(waves[2 * k, 4] + float(8 * m)) < NR / 2
                values = [jnp.where(inside, value, 0.0) for value in values]
            for part, value in enumerate(values):
                for side in range(2):
                    piece = value[:, side * LANES : (side + 1) * LANES]
                    if last:
                        final[part, side, 8 * m : 8 * m + 8] = piece
                    else:
                        images[target, side, part, 8 * m : 8 * m + 8, :] = piece

    block_of = iota((8, LANES), 1) // 16
    for part in range(2):
        for side in range(2):
            values = [final[part, side, pl.ds(i, 8, stride=8), :] for i in range(8)]
            for d in (4, 2, 1):
                clear = (block_of & d) == 0
                for i in range(8):
                    if i & d == 0:
                        a, b = values[i], values[i | d]
                        values[i] = jnp.where(clear, a, pltpu.roll(b, 16 * d, 1))
                        values[i | d] = jnp.where(clear, pltpu.roll(a, LANES - 16 * d, 1), b)
            for q in range(8):
                out_ref[side * 8 + q, part * 8 : part * 8 + 8, :] = values[q]


def invert_kernel(data, mixer_ref, out_ref):
    mixer = mixer_ref[...]
    for i in range(8):
        high, low = split(data[pl.ds(i, 2 * PASSES, stride=8), :])
        right_side = jnp.concatenate([high, low, high, jnp.zeros_like(high)], axis=0)
        tomo = jnp.dot(mixer, right_side.astype(BF16), preferred_element_type=F32)
        real, imag = tomo[:HEIGHTS], tomo[HEIGHTS:]
        out_ref[pl.ds(i, HEIGHTS, stride=8), :] = real * real + imag * imag


VMEM = pl.BlockSpec(memory_space=pltpu.VMEM)
HBM = pl.BlockSpec(memory_space=pltpu.HBM)
LIMIT = 16 << 20


def in_hbm(array):
    return pltpu.with_memory_space_constraint(array, pltpu.HBM)


def body(
    echo,
    chirp,
    pair_swap,
    range_shift,
    angle_shift,
    range_taps,
    angle_taps,
    phase_rates,
    invert,
    baseline_index,
):
    tables = (
        pair_swap,
        jnp.transpose(range_shift, (0, 2, 1)),
        jnp.transpose(angle_shift, (0, 2, 3, 1)),
        range_taps,
        angle_taps,
        jnp.transpose(phase_rates, (1, 2, 3, 0)),
    )
    tables = [in_hbm(table) for table in tables]
    held = [pltpu.SMEM(table.shape, table.dtype) for table in tables]
    params = pltpu.CompilerParams(vmem_limit_bytes=LIMIT)
    blocks = pl.pallas_call(
        compress_kernel,
        name="compress",
        out_shape=jax.ShapeDtypeStruct((N_AP // QUARTERS, QUARTERS, 2 * PULSES, LANES), F32),
        in_specs=[HBM] * 8,
        out_specs=HBM,
        scratch_shapes=[
            pltpu.VMEM((PULSES, 2, NS), BF16),
            pltpu.VMEM((2, TAPS), BF16),
            pltpu.VMEM((2 * PULSES, NS), F32),
            pltpu.VMEM((2, 2 * PULSES * BLOCKS, LANES), F32),
            pltpu.VMEM((2 * PULSES, 24 + BLOCKS, LANES), F32),
            pltpu.VMEM((2 * PULSES * FRAME_ROWS, LANES), F32),
            pltpu.VMEM((2, 2, TILES, PULSES, LANES), F32),
            pltpu.VMEM((QUARTERS, N_AP // QUARTERS, 2 * PULSES, LANES), F32),
            *held,
            pltpu.SemaphoreType.DMA((8 + QUARTERS,)),
        ],
        compiler_params=params,
        cost_estimate=pl.CostEstimate(flops=10**8, bytes_accessed=10**6, transcendentals=0),
    )(in_hbm(echo), in_hbm(chirp), *tables)
    weights, waves, taps, mixer = pl.pallas_call(
        tables_kernel,
        name="tables",
        out_shape=(
            jax.ShapeDtypeStruct((2 * CROSS, 2 * LANES, 2 * LANES), BF16),
            jax.ShapeDtypeStruct((2 * CROSS, 5, 8, 2 * LANES), F32),
            jax.ShapeDtypeStruct((2 * CROSS, KT, 8, LANES), F32),
            jax.ShapeDtypeStruct((2 * HEIGHTS, LANES), BF16),
        ),
        in_specs=[HBM] * 8,
        out_specs=(VMEM,) * 4,
        scratch_shapes=[
            pltpu.VMEM((2, BASES, HEIGHTS), F32),
            pltpu.SMEM((PASSES,), jnp.int32),
            *held,
            pltpu.SemaphoreType.DMA((8,)),
        ],
        compiler_params=params,
        cost_estimate=pl.CostEstimate(flops=10**8, bytes_accessed=10**6, transcendentals=0),
    )(*tables, in_hbm(jnp.transpose(invert, (0, 2, 1))), in_hbm(baseline_index))
    blocks = blocks.reshape(N_AP, 2 * PULSES, LANES)
    blocks = lax.all_to_all(blocks, "ap", split_axis=0, concat_axis=0, tiled=True)
    stacks = pl.pallas_call(
        merge_kernel,
        name="merge",
        out_shape=jax.ShapeDtypeStruct((PASSES, 16, LANES), F32),
        in_specs=[VMEM] * 4,
        out_specs=VMEM,
        scratch_shapes=[
            pltpu.VMEM((2, 2, 2, LANES, LANES), F32),
            pltpu.VMEM((2, 2, RW, LANES), F32),
        ],
        compiler_params=params,
        cost_estimate=pl.CostEstimate(flops=10**8, bytes_accessed=10**6, transcendentals=0),
    )(blocks, weights, waves, taps)
    stacks = lax.all_to_all(stacks, "pass", split_axis=0, concat_axis=0, tiled=True)
    power = pl.pallas_call(
        invert_kernel,
        name="invert",
        out_shape=jax.ShapeDtypeStruct((HEIGHTS * 8, LANES), F32),
        in_specs=[VMEM, VMEM],
        out_specs=VMEM,
        compiler_params=params,
        cost_estimate=pl.CostEstimate(flops=10**8, bytes_accessed=10**6, transcendentals=0),
    )(stacks.reshape(PASSES * 16, LANES), mixer)
    return power.reshape(1, HEIGHTS, 1, RW * BEAMS // PASSES)


def solution(mesh):
    return jax.shard_map(
        body,
        mesh=mesh,
        in_specs=(
            P("pass", "ap", None, None),
            P(),
            P("pass", None),
            P("pass", None, None),
            P("pass", None, None, None),
            P(),
            P(),
            P(),
            P(),
            P(),
        ),
        out_specs=P("pass", None, "ap", None),
        check_vma=False,
    )
```

```python
import math

import jax
import jax.numpy as jnp
from jax import lax
from jax.experimental import pallas as pl
from jax.experimental.pallas import tpu as pltpu
from jax.sharding import PartitionSpec as P

NR = 2048
TAPS = 1024
NS = 3072
HEIGHTS = 64
KT = 8
ORIGIN = KT // 2 - 1
RMAX = 16
BASES = 32
LEVELS = 8
LOCAL = 3
CROSS = 5
PULSES = 8
N_AP = 32
PASSES = 16
RW = 64
QUARTERS = 4
BEAMS = 256
LANES = 128
TILES = 17
BLOCKS = NR // LANES
FRAME_ROWS = 24
WINDOW = TAPS + LANES
SQRT_HALF = math.sqrt(0.5)
F32 = jnp.float32
BF16 = jnp.bfloat16

ROWS = (96, 88, 80, 72, 64)
FIRST_ROW = tuple(sum(ROWS[:k]) for k in range(CROSS))


def iota(shape, dim):
    return lax.broadcasted_iota(jnp.int32, shape, dim)


def sincos(x):
    turns = jnp.floor(x * (2.0 / math.pi) + 0.5)
    quadrant = turns.astype(jnp.int32)
    y = x - turns * 1.5703125
    y = y - turns * 4.837512969970703e-4
    y = y - turns * 7.54978995489188e-8
    y2 = y * y
    s = y * (1.0 + y2 * (-1.6666654611e-1 + y2 * (8.3321608736e-3 + y2 * -1.9515295891e-4)))
    c = 1.0 - 0.5 * y2 + y2 * y2 * (4.166664568298827e-2 + y2 * (-1.388731625493765e-3 + y2 * 2.443315711809948e-5))
    swap = (quadrant & 1) == 1
    cos_abs = jnp.where(swap, s, c)
    sin_abs = jnp.where(swap, c, s)
    cos = jnp.where(((quadrant + 1) & 2) == 2, -cos_abs, cos_abs)
    sin = jnp.where((quadrant & 2) == 2, -sin_abs, sin_abs)
    return cos, sin


def complex_mul(ar, ai, br, bi):
    return ar * br - ai * bi, ar * bi + ai * br


def reverse_bits(value):
    result = 0
    for digit in range(CROSS):
        result = result + (value // 2**digit % 2) * 2 ** (CROSS - 1 - digit)
    return result


def role(tables, level, child):
    flip = tables[0][0, level]
    return flip if child == 0 else 1 - flip


def step_offset(tables, level, child):
    return tables[1][0, role(tables, level, child), level] - ORIGIN


def slope_and_bend(tables, level, e, parity):
    rates = tables[5]
    slope = jnp.where(parity == 1, rates[e, 1, 0, level], rates[e, 0, 0, level])
    bend = jnp.where(parity == 1, rates[e, 1, 1, level], rates[e, 0, 1, level])
    return slope * (8.0 / NR), 8.0 * bend


def split(value):
    high = value.astype(BF16).astype(F32)
    return high, value - high


def start_copies(sources, targets, arrived):
    copies = [
        pltpu.make_async_copy(source, target, arrived.at[i])
        for i, (source, target) in enumerate(zip(sources, targets))
    ]
    for copy in copies:
        copy.start()
    return copies


def compress_kernel(
    echo_ref,
    chirp_ref,
    swap_ref,
    range_shift_ref,
    angle_shift_ref,
    range_taps_ref,
    angle_taps_ref,
    rates_ref,
    out_ref,
    echo,
    chirp,
    echo_rows,
    product,
    shifting,
    framed,
    images,
    outgoing,
    *scalars,
):
    *tables, arrived = scalars
    fetch_chirp = pltpu.make_async_copy(chirp_ref, chirp, arrived.at[len(tables)])
    fetch_chirp.start()
    fetch = pltpu.make_async_copy(echo_ref.at[0], echo, arrived.at[len(tables) + 1])
    fetch.start()
    fetch_tables = start_copies(
        (
            swap_ref,
            range_shift_ref,
            angle_shift_ref,
            range_taps_ref,
            angle_taps_ref,
            rates_ref,
        ),
        tables,
        arrived,
    )
    _, _, angle_shift_ref, range_taps_ref, angle_taps_ref, _ = tables
    rows8 = iota((PULSES, LANES), 0)
    lanes8 = iota((PULSES, LANES), 1)

    fetch_chirp.wait()
    bands = []
    row = iota((LANES, LANES), 0)
    column = iota((LANES, LANES), 1)
    for part in range(2):
        previous = jnp.zeros((LANES, LANES), F32)
        pieces = []
        for t in range(WINDOW // LANES):
            if t * LANES < TAPS:
                samples = chirp[part : part + 1, t * LANES : (t + 1) * LANES].astype(F32)
                current = pltpu.roll(
                    jnp.broadcast_to(samples, (LANES, LANES)), 0, 1, stride=1, stride_axis=0
                )
            else:
                current = jnp.zeros((LANES, LANES), F32)
            pieces.append(jnp.where(column >= row, current, previous).astype(BF16))
            previous = current
        bands.append(jnp.concatenate(pieces, axis=1))
    banded = jnp.concatenate(bands, axis=0)

    shifting[:, :8] = jnp.zeros((2 * PULSES, 8, LANES), F32)
    shifting[:, 8 + BLOCKS :] = jnp.zeros((2 * PULSES, 16, LANES), F32)

    fetch.wait()
    for n in range(PULSES):
        echo_rows[2 * n : 2 * n + 2, :] = echo[n].astype(F32)
    signal = echo_rows[...].astype(BF16)
    windows = jnp.concatenate(
        [signal[:, b * LANES : b * LANES + WINDOW] for b in range(BLOCKS)], axis=0
    )
    correlated = lax.dot_general(
        windows, banded, (((1,), (1,)), ((), ())), preferred_element_type=F32
    )
    for part in range(2):
        product[part] = correlated[:, part * LANES : (part + 1) * LANES]

    for copy in fetch_tables:
        copy.wait()

    position = lax.axis_index("ap")
    offset_above = jnp.int32(0)
    for level in range(LOCAL, LEVELS):
        bit = position // 2 ** (level - LOCAL) % 2
        offset_above = offset_above + jnp.where(
            bit == 1, step_offset(tables, level, 1), step_offset(tables, level, 0)
        )
    local_steps = [
        [step_offset(tables, level, child) for child in range(2)] for level in range(LOCAL)
    ]

    def prepare(level):
        beams = 2**level
        roles = [role(tables, level, child) for child in range(2)]
        in_child = rows8 >> level & 1
        tap_rows = [
            jnp.where(
                in_child == 1,
                range_taps_ref[level, roles[1], u],
                range_taps_ref[level, roles[0], u],
            )
            for u in range(KT)
        ]

        row16 = iota((2 * PULSES, LANES), 0)
        lane16 = iota((2 * PULSES, LANES), 1)
        of_child = row16 >> 3
        row_out = row16 & 7
        parity16 = row16 & 1

        def of_row(pick):
            return jnp.where(
                of_child == 1,
                jnp.where(parity16 == 1, pick(roles[1], 1), pick(roles[1], 0)),
                jnp.where(parity16 == 1, pick(roles[0], 1), pick(roles[0], 0)),
            )

        shift = of_row(lambda e, h: angle_shift_ref[0, e, h, level])
        beam = row_out % (2 * beams) // 2
        first = (row_out // (2 * beams) * 2 + of_child) * beams
        weights = jnp.zeros((2 * PULSES, LANES), F32)
        for u in range(KT):
            picked = first + jnp.clip(beam + (u - ORIGIN) + shift, 0, beams - 1)
            tap = of_row(lambda e, h: angle_taps_ref[level, e, h, u])
            weights = weights + jnp.where((lane16 & 7) == picked, tap, 0.0)
        high, low = split(weights)
        piece = lane16 >> 3
        left_side = jnp.where(piece < 2, high, jnp.where(piece == 2, low, 0.0)).astype(BF16)[:, :32]

        offset_out = jnp.full((PULSES, LANES), offset_above, jnp.int32)
        for later in range(level + 1, LOCAL):
            offset_out = offset_out + jnp.where(
                (rows8 >> later & 1) == 1, local_steps[later][1], local_steps[later][0]
            )
        cell_out = offset_out + lanes8
        beam_fraction = (rows8 % (2 * beams)).astype(F32) / (2.0 * beams)
        waves = []
        steps = []
        for child in range(2):
            slope, bend = slope_and_bend(tables, level, roles[child], rows8 & 1)
            cos, sin = sincos(slope * cell_out.astype(F32) + bend * beam_fraction)
            waves.append((cos * SQRT_HALF, sin * SQRT_HALF))
            steps.append(sincos(slope * float(LANES)))

        return tap_rows, left_side, cell_out, waves, steps

    totals = []
    for n in range(PULSES):
        total = offset_above
        for level in range(LOCAL):
            total = total + local_steps[level][n >> level & 1]
        totals.append(total)
        rest = total & (LANES - 1)
        even, odd = (
            [product[part, pl.ds(2 * n + i, BLOCKS, stride=16), :] for part in range(2)]
            for i in range(2)
        )
        for part, value in enumerate((even[0] + odd[1], odd[0] - even[1])):
            shifting[2 * n + part, 8 : 8 + BLOCKS] = pltpu.roll(
                value, (LANES - rest) & (LANES - 1), 1
            )
    lane = iota((FRAME_ROWS, LANES), 1)
    for n in range(PULSES):
        whole = totals[n] >> 7
        keep = lane < LANES - (totals[n] & (LANES - 1))
        for part in range(2):
            i = 2 * n + part
            left = shifting[i, pl.ds(8 + whole, FRAME_ROWS), :]
            right = shifting[i, pl.ds(9 + whole, FRAME_ROWS), :]
            framed[i * FRAME_ROWS : (i + 1) * FRAME_ROWS] = jnp.where(keep, left, right)

    sends = []

    def send(window, values):
        block = reverse_bits(window)
        for part in range(2):
            outgoing[block % QUARTERS, block // QUARTERS, part * 8 : part * 8 + 8] = values[part]
        if (window + 1) % (N_AP // QUARTERS) == 0:
            quarter = block % QUARTERS
            sends.append(
                pltpu.make_async_copy(
                    outgoing.at[quarter], out_ref.at[:, quarter], arrived.at[8 + quarter]
                )
            )
            sends[-1].start()

    def load(level, part, b):
        if level == 0:
            return framed[pl.ds(part * FRAME_ROWS + b, PULSES, stride=2 * FRAME_ROWS), :]
        return images[level % 2, part, b]

    for level in range(LOCAL):
        tap_rows, left_side, cell_out, waves, steps = prepare(level)

        def turn(value, cells):
            return pltpu.roll(value, LANES - cells, 1)

        def moved(here, there, cells):
            return jnp.where(lanes8 < LANES - cells, here, there)

        def rolls(b):
            values = [load(level, part, b) for part in range(2)]
            return [[value] + [turn(value, u) for u in (1, 2, 3)] for value in values]

        def runs(here, there):
            found = []
            for part in range(2):
                value = here[part][0]
                near, far = tap_rows[0] * value, tap_rows[4] * value
                for u in (1, 2, 3):
                    value = moved(here[part][u], there[part][u], u)
                    near = near + tap_rows[u] * value
                    far = far + tap_rows[4 + u] * value
                found.append((near, turn(far, 4)))
            return found

        here = rolls(0)
        there = rolls(1)
        sums = runs(here, there)
        for b in range(TILES):
            if b + 1 < TILES:
                here, there = there, rolls(b + 2) if b + 2 < TILES else there
                sums_there = runs(here, there)
            pieces = []
            for part in range(2):
                total = sums[part][0] + moved(sums[part][1], sums_there[part][1], 4)
                high, low = split(total)
                pieces.append(
                    jnp.concatenate([high, low, high, jnp.zeros((PULSES, LANES), F32)], axis=0)
                )
            sums = sums_there
            right_side = jnp.concatenate(pieces, axis=1).astype(BF16)
            steered = jnp.dot(left_side, right_side, preferred_element_type=F32)
            terms = []
            for child in range(2):
                rows = steered[child * PULSES : (child + 1) * PULSES]
                terms.append(complex_mul(*waves[child], rows[:, :LANES], rows[:, LANES:]))
                waves[child] = complex_mul(*waves[child], *steps[child])
            values = [a + c for a, c in zip(*terms)]
            if b * LANES < LEVELS * (RMAX + ORIGIN) or (b + 1) * LANES > NR - LEVELS * RMAX:
                where_r = cell_out + b * LANES
                inside = (where_r >= 0) & (where_r < NR)
                values = [jnp.where(inside, value, 0.0) for value in values]
            if level + 1 < LOCAL:
                for part in range(2):
                    images[(level + 1) % 2, part, b] = values[part]
            else:
                turned = [pltpu.roll(value, RW, 1) for value in values]
                if b > 0:
                    joined = [jnp.where(lanes8 < RW, a, c) for a, c in zip(before, turned)]
                    send(2 * b - 1, joined)
                if b < BLOCKS:
                    send(2 * b, values)
                before = turned
    for copy in sends:
        copy.wait()


def column_offset(tables, level, column):
    offset = jnp.zeros_like(column)
    for later in range(level + 1, LEVELS):
        bit = column >> (7 - (later - level - 1)) & 1
        offset = offset + jnp.where(
            bit == 1, step_offset(tables, later, 1), step_offset(tables, later, 0)
        )
    return offset


def tables_kernel(
    swap_ref,
    range_shift_ref,
    angle_shift_ref,
    range_taps_ref,
    angle_taps_ref,
    rates_ref,
    invert_ref,
    baseline_ref,
    weights_ref,
    waves_ref,
    taps_ref,
    mixer_ref,
    invert,
    baseline,
    *scalars,
):
    *tables, arrived = scalars
    for copy in start_copies(
        (
            swap_ref,
            range_shift_ref,
            angle_shift_ref,
            range_taps_ref,
            angle_taps_ref,
            rates_ref,
            invert_ref,
            baseline_ref,
        ),
        (*tables, invert, baseline),
        arrived,
    ):
        copy.wait()
    _, _, angle_shift_ref, range_taps_ref, angle_taps_ref, _ = tables
    position = lax.axis_index("ap")
    base = reverse_bits(position) * RW
    column = iota((1, 2 * LANES), 1)
    row = iota((LANES, 2 * LANES), 0)
    parity = column & 1
    for k in range(CROSS):
        level = LOCAL + k
        first_wave = FIRST_ROW[k]
        beams = 2**level
        beam = column % (2 * beams) // 2
        first_row = column // (2 * beams) * beams
        beam_fraction = (column % (2 * beams)).astype(F32) / (2.0 * beams)
        cell = iota((8, 2 * LANES), 0) + (base + column_offset(tables, level, column))
        centred = cell.astype(F32) - (NR - 1) / 2
        for child in range(2):
            e = role(tables, level, child)
            shift = jnp.where(
                parity == 1, angle_shift_ref[0, e, 1, level], angle_shift_ref[0, e, 0, level]
            )
            weights = jnp.zeros((LANES, 2 * LANES), F32)
            for u in range(KT):
                tap = jnp.where(
                    parity == 1, angle_taps_ref[level, e, 1, u], angle_taps_ref[level, e, 0, u]
                )
                picked = first_row + jnp.clip(beam + (u - ORIGIN) + shift, 0, beams - 1)
                weights = weights + jnp.where(row == picked, tap, 0.0)
            high, low = split(weights)
            at = 2 * k + child
            weights_ref[at, :LANES] = high.astype(BF16)
            weights_ref[at, LANES:] = low.astype(BF16)
            slope, bend = slope_and_bend(tables, level, e, parity)
            cos, sin = sincos(slope * cell.astype(F32) + bend * beam_fraction)
            wave = (cos * SQRT_HALF, sin * SQRT_HALF)
            step = sincos(jnp.broadcast_to(slope * 8.0, (8, 2 * LANES)))
            for m in range(ROWS[k] // 8):
                inside = jnp.abs(centred + float(8 * m)) < NR / 2
                for part in range(2):
                    waves_ref[child, part, first_wave + 8 * m : first_wave + 8 * m + 8] = (
                        jnp.where(inside, wave[part], 0.0)
                    )
                wave = complex_mul(*wave, *step)
            for u in range(KT):
                taps_ref[at, u : u + 1] = jnp.full((1, LANES), range_taps_ref[level, e, u], F32)

    lane = iota((1, LANES), 1)
    wanted = jnp.zeros((1, LANES), jnp.int32)
    for p in range(PASSES):
        wanted = jnp.where(lane % (2 * PASSES) // 2 == p, baseline[p], wanted)
    chosen = (iota((BASES, LANES), 0) == wanted).astype(F32)
    steer = [
        lax.dot_general(
            invert[part],
            chosen,
            (((0,), (0,)), ((), ())),
            precision=lax.Precision.HIGHEST,
            preferred_element_type=F32,
        )
        for part in range(2)
    ]
    imaginary = (lane & 1) == 1
    high, low = split(
        jnp.concatenate(
            [jnp.where(imaginary, -steer[1], steer[0]), jnp.where(imaginary, steer[0], steer[1])],
            axis=0,
        )
    )
    piece = lane // (2 * PASSES)
    mixer_ref[...] = jnp.where(piece < 2, high, jnp.where(piece == 2, low, 0.0)).astype(BF16)


def merge_kernel(
    blocks,
    weights,
    waves,
    taps,
    out_ref,
    images,
    final,
):
    for child in range(2):
        order = []
        for i in range(N_AP // 2):
            order.append(
                child + 2 * (i >> 3 & 1) + 4 * (i >> 2 & 1) + 8 * (i >> 1 & 1) + 16 * (i & 1)
            )
        for part in range(2):
            stacked = jnp.concatenate(
                [blocks[g, part * PULSES : (part + 1) * PULSES, :] for g in order], axis=0
            )
            images[0, child, part] = stacked.T

    for k in range(CROSS):
        rows = ROWS[k]
        source, target = k % 2, 1 - k % 2
        last = k == CROSS - 1
        steered = []
        for child in range(2):
            tap = [
                jnp.broadcast_to(taps[2 * k + child, u : u + 1], (rows, LANES)) for u in range(KT)
            ]
            parts = []
            for part in range(2):
                total = tap[0] * images[source, child, part, 0:rows, :]
                for u in range(1, KT):
                    total = total + tap[u] * images[source, child, part, u : u + rows, :]
                parts.append(total)
            ranged = jnp.concatenate(parts, axis=0)
            high = ranged.astype(BF16)
            low = (ranged - high.astype(F32)).astype(BF16)
            matrix = weights[2 * k + child]
            steered.append(
                jnp.dot(
                    jnp.concatenate([high, low, high], axis=1),
                    jnp.concatenate([matrix[:LANES], matrix[:LANES], matrix[LANES:]], axis=0),
                    preferred_element_type=F32,
                )
            )
        for m in range(rows // 8):
            at = FIRST_ROW[k] + 8 * m
            terms = [
                complex_mul(
                    waves[child, 0, at : at + 8],
                    waves[child, 1, at : at + 8],
                    steered[child][8 * m : 8 * m + 8],
                    steered[child][rows + 8 * m : rows + 8 * m + 8],
                )
                for child in range(2)
            ]
            values = [a + c for a, c in zip(*terms)]
            for part, value in enumerate(values):
                for side in range(2):
                    piece = value[:, side * LANES : (side + 1) * LANES]
                    if last:
                        final[part, side, 8 * m : 8 * m + 8] = piece
                    else:
                        images[target, side, part, 8 * m : 8 * m + 8, :] = piece

    block_of = iota((8, LANES), 1) // 16
    for part in range(2):
        for side in range(2):
            values = [final[part, side, pl.ds(i, 8, stride=8), :] for i in range(8)]
            for d in (4, 2, 1):
                clear = (block_of & d) == 0
                for i in range(8):
                    if i & d == 0:
                        a, b = values[i], values[i | d]
                        values[i] = jnp.where(clear, a, pltpu.roll(b, 16 * d, 1))
                        values[i | d] = jnp.where(clear, pltpu.roll(a, LANES - 16 * d, 1), b)
            for q in range(8):
                out_ref[side * 8 + q, part * 8 : part * 8 + 8, :] = values[q]


def invert_kernel(data, mixer_ref, out_ref):
    mixer = mixer_ref[...]
    for i in range(8):
        high, low = split(data[pl.ds(i, 2 * PASSES, stride=8), :])
        right_side = jnp.concatenate([high, low, high, jnp.zeros_like(high)], axis=0)
        tomo = jnp.dot(mixer, right_side.astype(BF16), preferred_element_type=F32)
        real, imag = tomo[:HEIGHTS], tomo[HEIGHTS:]
        out_ref[pl.ds(i, HEIGHTS, stride=8), :] = real * real + imag * imag


VMEM = pl.BlockSpec(memory_space=pltpu.VMEM)
HBM = pl.BlockSpec(memory_space=pltpu.HBM)
LIMIT = 16 << 20


def in_hbm(array):
    return pltpu.with_memory_space_constraint(array, pltpu.HBM)


def body(
    echo,
    chirp,
    pair_swap,
    range_shift,
    angle_shift,
    range_taps,
    angle_taps,
    phase_rates,
    invert,
    baseline_index,
):
    tables = (
        pair_swap,
        jnp.transpose(range_shift, (0, 2, 1)),
        jnp.transpose(angle_shift, (0, 2, 3, 1)),
        range_taps,
        angle_taps,
        jnp.transpose(phase_rates, (1, 2, 3, 0)),
    )
    tables = [in_hbm(table) for table in tables]
    held = [pltpu.SMEM(table.shape, table.dtype) for table in tables]
    params = pltpu.CompilerParams(vmem_limit_bytes=LIMIT)
    blocks = pl.pallas_call(
        compress_kernel,
        name="compress",
        out_shape=jax.ShapeDtypeStruct((N_AP // QUARTERS, QUARTERS, 2 * PULSES, LANES), F32),
        in_specs=[HBM] * 8,
        out_specs=HBM,
        scratch_shapes=[
            pltpu.VMEM((PULSES, 2, NS), BF16),
            pltpu.VMEM((2, TAPS), BF16),
            pltpu.VMEM((2 * PULSES, NS), F32),
            pltpu.VMEM((2, 2 * PULSES * BLOCKS, LANES), F32),
            pltpu.VMEM((2 * PULSES, 24 + BLOCKS, LANES), F32),
            pltpu.VMEM((2 * PULSES * FRAME_ROWS, LANES), F32),
            pltpu.VMEM((2, 2, TILES, PULSES, LANES), F32),
            pltpu.VMEM((QUARTERS, N_AP // QUARTERS, 2 * PULSES, LANES), F32),
            *held,
            pltpu.SemaphoreType.DMA((8 + QUARTERS,)),
        ],
        compiler_params=params,
        cost_estimate=pl.CostEstimate(flops=10**8, bytes_accessed=10**6, transcendentals=0),
    )(in_hbm(echo), in_hbm(chirp), *tables)
    weights, waves, taps, mixer = pl.pallas_call(
        tables_kernel,
        name="tables",
        out_shape=(
            jax.ShapeDtypeStruct((2 * CROSS, 2 * LANES, 2 * LANES), BF16),
            jax.ShapeDtypeStruct((2, 2, sum(ROWS), 2 * LANES), F32),
            jax.ShapeDtypeStruct((2 * CROSS, KT, LANES), F32),
            jax.ShapeDtypeStruct((2 * HEIGHTS, LANES), BF16),
        ),
        in_specs=[HBM] * 8,
        out_specs=(VMEM,) * 4,
        scratch_shapes=[
            pltpu.VMEM((2, BASES, HEIGHTS), F32),
            pltpu.SMEM((PASSES,), jnp.int32),
            *held,
            pltpu.SemaphoreType.DMA((8,)),
        ],
        compiler_params=params,
        cost_estimate=pl.CostEstimate(flops=10**8, bytes_accessed=10**6, transcendentals=0),
    )(*tables, in_hbm(jnp.transpose(invert, (0, 2, 1))), in_hbm(baseline_index))
    blocks = blocks.reshape(N_AP, 2 * PULSES, LANES)
    blocks = lax.all_to_all(blocks, "ap", split_axis=0, concat_axis=0, tiled=True)
    stacks = pl.pallas_call(
        merge_kernel,
        name="merge",
        out_shape=jax.ShapeDtypeStruct((PASSES, 16, LANES), F32),
        in_specs=[VMEM] * 4,
        out_specs=VMEM,
        scratch_shapes=[
            pltpu.VMEM((2, 2, 2, LANES, LANES), F32),
            pltpu.VMEM((2, 2, RW, LANES), F32),
        ],
        compiler_params=params,
        cost_estimate=pl.CostEstimate(flops=10**8, bytes_accessed=10**6, transcendentals=0),
    )(blocks, weights, waves, taps)
    stacks = lax.all_to_all(stacks, "pass", split_axis=0, concat_axis=0, tiled=True)
    power = pl.pallas_call(
        invert_kernel,
        name="invert",
        out_shape=jax.ShapeDtypeStruct((HEIGHTS * 8, LANES), F32),
        in_specs=[VMEM, VMEM],
        out_specs=VMEM,
        compiler_params=params,
        cost_estimate=pl.CostEstimate(flops=10**8, bytes_accessed=10**6, transcendentals=0),
    )(stacks.reshape(PASSES * 16, LANES), mixer)
    return power.reshape(1, HEIGHTS, 1, RW * BEAMS // PASSES)


def solution(mesh):
    return jax.shard_map(
        body,
        mesh=mesh,
        in_specs=(
            P("pass", "ap", None, None),
            P(),
            P("pass", None),
            P("pass", None, None),
            P("pass", None, None, None),
            P(),
            P(),
            P(),
            P(),
            P(),
        ),
        out_specs=P("pass", None, "ap", None),
        check_vma=False,
    )
```

```python
import math

import jax
import jax.numpy as jnp
from jax import lax
from jax.experimental import pallas as pl
from jax.experimental.pallas import tpu as pltpu
from jax.sharding import PartitionSpec as P

NR = 2048
TAPS = 1024
NS = 3072
HEIGHTS = 64
KT = 8
ORIGIN = KT // 2 - 1
RMAX = 16
BASES = 32
LEVELS = 8
LOCAL = 3
CROSS = 5
PULSES = 8
N_AP = 32
PASSES = 16
RW = 64
QUARTERS = 4
AP_FIRST = 20
PASS_FIRST = 12
BEAMS = 256
LANES = 128
TILES = 17
BLOCKS = NR // LANES
FRAME_ROWS = 24
WINDOW = TAPS + LANES
SQRT_HALF = math.sqrt(0.5)
F32 = jnp.float32
BF16 = jnp.bfloat16

ROWS = (96, 88, 80, 72, 64)


def iota(shape, dim):
    return lax.broadcasted_iota(jnp.int32, shape, dim)


def sincos(x):
    turns = jnp.floor(x * (2.0 / math.pi) + 0.5)
    quadrant = turns.astype(jnp.int32)
    y = x - turns * 1.5703125
    y = y - turns * 4.837512969970703e-4
    y = y - turns * 7.54978995489188e-8
    y2 = y * y
    s = y * (1.0 + y2 * (-1.6666654611e-1 + y2 * (8.3321608736e-3 + y2 * -1.9515295891e-4)))
    c = 1.0 - 0.5 * y2 + y2 * y2 * (4.166664568298827e-2 + y2 * (-1.388731625493765e-3 + y2 * 2.443315711809948e-5))
    swap = (quadrant & 1) == 1
    cos_abs = jnp.where(swap, s, c)
    sin_abs = jnp.where(swap, c, s)
    cos = jnp.where(((quadrant + 1) & 2) == 2, -cos_abs, cos_abs)
    sin = jnp.where((quadrant & 2) == 2, -sin_abs, sin_abs)
    return cos, sin


def complex_mul(ar, ai, br, bi):
    return ar * br - ai * bi, ar * bi + ai * br


def reverse_bits(value):
    result = 0
    for digit in range(CROSS):
        result = result + (value // 2**digit % 2) * 2 ** (CROSS - 1 - digit)
    return result


def role(tables, level, child):
    flip = tables[0][0, level]
    return flip if child == 0 else 1 - flip


def step_offset(tables, level, child):
    return tables[1][0, role(tables, level, child), level] - ORIGIN


def slope_and_bend(tables, level, e, parity):
    rates = tables[5]
    slope = jnp.where(parity == 1, rates[e, 1, 0, level], rates[e, 0, 0, level])
    bend = jnp.where(parity == 1, rates[e, 1, 1, level], rates[e, 0, 1, level])
    return slope * (8.0 / NR), 8.0 * bend


def split(value):
    high = value.astype(BF16).astype(F32)
    return high, value - high


def start_copies(sources, targets, arrived):
    copies = [
        pltpu.make_async_copy(source, target, arrived.at[i])
        for i, (source, target) in enumerate(zip(sources, targets))
    ]
    for copy in copies:
        copy.start()
    return copies


def compress_kernel(
    echo_ref,
    chirp_ref,
    swap_ref,
    range_shift_ref,
    angle_shift_ref,
    range_taps_ref,
    angle_taps_ref,
    rates_ref,
    out_ref,
    echo,
    chirp,
    echo_rows,
    product,
    shifting,
    framed,
    images,
    outgoing,
    *scalars,
):
    *tables, arrived = scalars
    fetch_chirp = pltpu.make_async_copy(chirp_ref, chirp, arrived.at[len(tables)])
    fetch_chirp.start()
    fetch = pltpu.make_async_copy(echo_ref.at[0], echo, arrived.at[len(tables) + 1])
    fetch.start()
    fetch_tables = start_copies(
        (
            swap_ref,
            range_shift_ref,
            angle_shift_ref,
            range_taps_ref,
            angle_taps_ref,
            rates_ref,
        ),
        tables,
        arrived,
    )
    _, _, angle_shift_ref, range_taps_ref, angle_taps_ref, _ = tables
    rows8 = iota((PULSES, LANES), 0)
    lanes8 = iota((PULSES, LANES), 1)

    fetch_chirp.wait()
    bands = []
    row = iota((LANES, LANES), 0)
    column = iota((LANES, LANES), 1)
    for part in range(2):
        previous = jnp.zeros((LANES, LANES), F32)
        pieces = []
        for t in range(WINDOW // LANES):
            if t * LANES < TAPS:
                samples = chirp[part : part + 1, t * LANES : (t + 1) * LANES].astype(F32)
                current = pltpu.roll(
                    jnp.broadcast_to(samples, (LANES, LANES)), 0, 1, stride=1, stride_axis=0
                )
            else:
                current = jnp.zeros((LANES, LANES), F32)
            pieces.append(jnp.where(column >= row, current, previous).astype(BF16))
            previous = current
        bands.append(jnp.concatenate(pieces, axis=1))
    banded = jnp.concatenate(bands, axis=0)

    shifting[:, :8] = jnp.zeros((2 * PULSES, 8, LANES), F32)
    shifting[:, 8 + BLOCKS :] = jnp.zeros((2 * PULSES, 16, LANES), F32)

    fetch.wait()
    for n in range(PULSES):
        echo_rows[2 * n : 2 * n + 2, :] = echo[n].astype(F32)
    signal = echo_rows[...].astype(BF16)
    windows = jnp.concatenate(
        [signal[:, b * LANES : b * LANES + WINDOW] for b in range(BLOCKS)], axis=0
    )
    correlated = lax.dot_general(
        windows, banded, (((1,), (1,)), ((), ())), preferred_element_type=F32
    )
    for part in range(2):
        product[part] = correlated[:, part * LANES : (part + 1) * LANES]

    for copy in fetch_tables:
        copy.wait()

    position = lax.axis_index("ap")
    offset_above = jnp.int32(0)
    for level in range(LOCAL, LEVELS):
        bit = position // 2 ** (level - LOCAL) % 2
        offset_above = offset_above + jnp.where(
            bit == 1, step_offset(tables, level, 1), step_offset(tables, level, 0)
        )
    local_steps = [
        [step_offset(tables, level, child) for child in range(2)] for level in range(LOCAL)
    ]

    def prepare(level):
        beams = 2**level
        roles = [role(tables, level, child) for child in range(2)]
        in_child = rows8 >> level & 1
        tap_rows = [
            jnp.where(
                in_child == 1,
                range_taps_ref[level, roles[1], u],
                range_taps_ref[level, roles[0], u],
            )
            for u in range(KT)
        ]

        row16 = iota((2 * PULSES, LANES), 0)
        lane16 = iota((2 * PULSES, LANES), 1)
        of_child = row16 >> 3
        row_out = row16 & 7
        parity16 = row16 & 1

        def of_row(pick):
            return jnp.where(
                of_child == 1,
                jnp.where(parity16 == 1, pick(roles[1], 1), pick(roles[1], 0)),
                jnp.where(parity16 == 1, pick(roles[0], 1), pick(roles[0], 0)),
            )

        shift = of_row(lambda e, h: angle_shift_ref[0, e, h, level])
        beam = row_out % (2 * beams) // 2
        first = (row_out // (2 * beams) * 2 + of_child) * beams
        weights = jnp.zeros((2 * PULSES, LANES), F32)
        for u in range(KT):
            picked = first + jnp.clip(beam + (u - ORIGIN) + shift, 0, beams - 1)
            tap = of_row(lambda e, h: angle_taps_ref[level, e, h, u])
            weights = weights + jnp.where((lane16 & 7) == picked, tap, 0.0)
        high, low = split(weights)
        piece = lane16 >> 3
        left_side = jnp.where(piece < 2, high, jnp.where(piece == 2, low, 0.0)).astype(BF16)[:, :32]

        offset_out = jnp.full((PULSES, LANES), offset_above, jnp.int32)
        for later in range(level + 1, LOCAL):
            offset_out = offset_out + jnp.where(
                (rows8 >> later & 1) == 1, local_steps[later][1], local_steps[later][0]
            )
        cell_out = offset_out + lanes8
        beam_fraction = (rows8 % (2 * beams)).astype(F32) / (2.0 * beams)
        waves = []
        steps = []
        for child in range(2):
            slope, bend = slope_and_bend(tables, level, roles[child], rows8 & 1)
            cos, sin = sincos(slope * cell_out.astype(F32) + bend * beam_fraction)
            waves.append((cos * SQRT_HALF, sin * SQRT_HALF))
            steps.append(sincos(slope * float(LANES)))

        return tap_rows, left_side, cell_out, waves, steps

    totals = []
    for n in range(PULSES):
        total = offset_above
        for level in range(LOCAL):
            total = total + local_steps[level][n >> level & 1]
        totals.append(total)
        rest = total & (LANES - 1)
        even, odd = (
            [product[part, pl.ds(2 * n + i, BLOCKS, stride=16), :] for part in range(2)]
            for i in range(2)
        )
        for part, value in enumerate((even[0] + odd[1], odd[0] - even[1])):
            shifting[2 * n + part, 8 : 8 + BLOCKS] = pltpu.roll(
                value, (LANES - rest) & (LANES - 1), 1
            )
    lane = iota((FRAME_ROWS, LANES), 1)
    for n in range(PULSES):
        whole = totals[n] >> 7
        keep = lane < LANES - (totals[n] & (LANES - 1))
        for part in range(2):
            i = 2 * n + part
            left = shifting[i, pl.ds(8 + whole, FRAME_ROWS), :]
            right = shifting[i, pl.ds(9 + whole, FRAME_ROWS), :]
            framed[i * FRAME_ROWS : (i + 1) * FRAME_ROWS] = jnp.where(keep, left, right)

    sends = []

    def send(window, values):
        block = reverse_bits(window) ^ AP_FIRST
        for part in range(2):
            outgoing[block % QUARTERS, block // QUARTERS, part * 8 : part * 8 + 8] = values[part]
        if (window + 1) % (N_AP // QUARTERS) == 0:
            quarter = block % QUARTERS
            sends.append(
                pltpu.make_async_copy(
                    outgoing.at[quarter], out_ref.at[:, quarter], arrived.at[8 + quarter]
                )
            )
            sends[-1].start()

    def load(level, part, b):
        if level == 0:
            return framed[pl.ds(part * FRAME_ROWS + b, PULSES, stride=2 * FRAME_ROWS), :]
        return images[level % 2, part, b]

    for level in range(LOCAL):
        tap_rows, left_side, cell_out, waves, steps = prepare(level)

        def turn(value, cells):
            return pltpu.roll(value, LANES - cells, 1)

        def moved(here, there, cells):
            return jnp.where(lanes8 < LANES - cells, here, there)

        def rolls(b):
            values = [load(level, part, b) for part in range(2)]
            return [[value] + [turn(value, u) for u in (1, 2, 3)] for value in values]

        def runs(here, there):
            found = []
            for part in range(2):
                value = here[part][0]
                near, far = tap_rows[0] * value, tap_rows[4] * value
                for u in (1, 2, 3):
                    value = moved(here[part][u], there[part][u], u)
                    near = near + tap_rows[u] * value
                    far = far + tap_rows[4 + u] * value
                found.append((near, turn(far, 4)))
            return found

        here = rolls(0)
        there = rolls(1)
        sums = runs(here, there)
        for b in range(TILES):
            if b + 1 < TILES:
                here, there = there, rolls(b + 2) if b + 2 < TILES else there
                sums_there = runs(here, there)
            pieces = []
            for part in range(2):
                total = sums[part][0] + moved(sums[part][1], sums_there[part][1], 4)
                high, low = split(total)
                pieces.append(
                    jnp.concatenate([high, low, high, jnp.zeros((PULSES, LANES), F32)], axis=0)
                )
            sums = sums_there
            right_side = jnp.concatenate(pieces, axis=1).astype(BF16)
            steered = jnp.dot(left_side, right_side, preferred_element_type=F32)
            terms = []
            for child in range(2):
                rows = steered[child * PULSES : (child + 1) * PULSES]
                terms.append(complex_mul(*waves[child], rows[:, :LANES], rows[:, LANES:]))
                waves[child] = complex_mul(*waves[child], *steps[child])
            values = [a + c for a, c in zip(*terms)]
            if b * LANES < LEVELS * (RMAX + ORIGIN) or (b + 1) * LANES > NR - LEVELS * RMAX:
                where_r = cell_out + b * LANES
                inside = (where_r >= 0) & (where_r < NR)
                values = [jnp.where(inside, value, 0.0) for value in values]
            if level + 1 < LOCAL:
                for part in range(2):
                    images[(level + 1) % 2, part, b] = values[part]
            else:
                turned = [pltpu.roll(value, RW, 1) for value in values]
                if b > 0:
                    joined = [jnp.where(lanes8 < RW, a, c) for a, c in zip(before, turned)]
                    send(2 * b - 1, joined)
                if b < BLOCKS:
                    send(2 * b, values)
                before = turned
    for copy in sends:
        copy.wait()


def column_offset(tables, level, column):
    offset = jnp.zeros_like(column)
    for later in range(level + 1, LEVELS):
        bit = column >> (7 - (later - level - 1)) & 1
        offset = offset + jnp.where(
            bit == 1, step_offset(tables, later, 1), step_offset(tables, later, 0)
        )
    return offset


def tables_kernel(
    swap_ref,
    range_shift_ref,
    angle_shift_ref,
    range_taps_ref,
    angle_taps_ref,
    rates_ref,
    invert_ref,
    baseline_ref,
    weights_ref,
    waves_ref,
    taps_ref,
    mixer_ref,
    invert,
    baseline,
    *scalars,
):
    *tables, arrived = scalars
    for copy in start_copies(
        (
            swap_ref,
            range_shift_ref,
            angle_shift_ref,
            range_taps_ref,
            angle_taps_ref,
            rates_ref,
            invert_ref,
            baseline_ref,
        ),
        (*tables, invert, baseline),
        arrived,
    ):
        copy.wait()
    _, _, angle_shift_ref, range_taps_ref, angle_taps_ref, _ = tables
    position = lax.axis_index("ap")
    base = reverse_bits(position) * RW
    column = iota((1, 2 * LANES), 1)
    row = iota((LANES, 2 * LANES), 0)
    parity = column & 1
    for k in range(CROSS):
        level = LOCAL + k
        beams = 2**level
        beam = column % (2 * beams) // 2
        first_row = column // (2 * beams) * beams
        beam_fraction = (column % (2 * beams)).astype(F32) / (2.0 * beams)
        cell = iota((8, 2 * LANES), 0) + (base + column_offset(tables, level, column))
        for child in range(2):
            e = role(tables, level, child)
            shift = jnp.where(
                parity == 1, angle_shift_ref[0, e, 1, level], angle_shift_ref[0, e, 0, level]
            )
            weights = jnp.zeros((LANES, 2 * LANES), F32)
            for u in range(KT):
                tap = jnp.where(
                    parity == 1, angle_taps_ref[level, e, 1, u], angle_taps_ref[level, e, 0, u]
                )
                picked = first_row + jnp.clip(beam + (u - ORIGIN) + shift, 0, beams - 1)
                weights = weights + jnp.where(row == picked, tap, 0.0)
            high, low = split(weights)
            at = 2 * k + child
            weights_ref[at, :LANES] = high.astype(BF16)
            weights_ref[at, LANES:] = low.astype(BF16)
            slope, bend = slope_and_bend(tables, level, e, parity)
            cos, sin = sincos(slope * cell.astype(F32) + bend * beam_fraction)
            waves_ref[at, 0] = cos * SQRT_HALF
            waves_ref[at, 1] = sin * SQRT_HALF
            cos, sin = sincos(jnp.broadcast_to(slope * 8.0, (8, 2 * LANES)))
            waves_ref[at, 2] = cos
            waves_ref[at, 3] = sin
            waves_ref[at, 4] = cell.astype(F32) - (NR - 1) / 2
            for u in range(KT):
                taps_ref[at, u] = jnp.full((8, LANES), range_taps_ref[level, e, u], F32)

    lane = iota((1, LANES), 1)
    wanted = jnp.zeros((1, LANES), jnp.int32)
    for p in range(PASSES):
        wanted = jnp.where(lane % (2 * PASSES) // 2 == p ^ PASS_FIRST, baseline[p], wanted)
    chosen = (iota((BASES, LANES), 0) == wanted).astype(F32)
    steer = [
        lax.dot_general(
            invert[part],
            chosen,
            (((0,), (0,)), ((), ())),
            precision=lax.Precision.HIGHEST,
            preferred_element_type=F32,
        )
        for part in range(2)
    ]
    imaginary = (lane & 1) == 1
    high, low = split(
        jnp.concatenate(
            [jnp.where(imaginary, -steer[1], steer[0]), jnp.where(imaginary, steer[0], steer[1])],
            axis=0,
        )
    )
    piece = lane // (2 * PASSES)
    mixer_ref[...] = jnp.where(piece < 2, high, jnp.where(piece == 2, low, 0.0)).astype(BF16)


def merge_kernel(
    blocks,
    weights,
    waves,
    taps,
    out_ref,
    images,
    final,
):
    for child in range(2):
        order = []
        for i in range(N_AP // 2):
            order.append(
                child + 2 * (i >> 3 & 1) + 4 * (i >> 2 & 1) + 8 * (i >> 1 & 1) + 16 * (i & 1)
            )
        for part in range(2):
            stacked = jnp.concatenate(
                [blocks[g ^ AP_FIRST, part * PULSES : (part + 1) * PULSES, :] for g in order], axis=0
            )
            images[0, child, part] = stacked.T

    for k in range(CROSS):
        rows = ROWS[k]
        source, target = k % 2, 1 - k % 2
        last = k == CROSS - 1
        steered = []
        for child in range(2):
            tap = [
                jnp.concatenate([taps[2 * k + child, u]] * (rows // 8), axis=0) for u in range(KT)
            ]
            parts = []
            for part in range(2):
                total = tap[0] * images[source, child, part, 0:rows, :]
                for u in range(1, KT):
                    total = total + tap[u] * images[source, child, part, u : u + rows, :]
                parts.append(total)
            ranged = jnp.concatenate(parts, axis=0)
            high = ranged.astype(BF16)
            low = (ranged - high.astype(F32)).astype(BF16)
            matrix = weights[2 * k + child]
            steered.append(
                jnp.dot(
                    jnp.concatenate([high, low, high], axis=1),
                    jnp.concatenate([matrix[:LANES], matrix[:LANES], matrix[LANES:]], axis=0),
                    preferred_element_type=F32,
                )
            )
        turning = [(waves[2 * k + child, 0], waves[2 * k + child, 1]) for child in range(2)]
        steps = [(waves[2 * k + child, 2], waves[2 * k + child, 3]) for child in range(2)]
        for m in range(rows // 8):
            terms = []
            for child in range(2):
                terms.append(
                    complex_mul(
                        *turning[child],
                        steered[child][8 * m : 8 * m + 8],
                        steered[child][rows + 8 * m : rows + 8 * m + 8],
                    )
                )
                turning[child] = complex_mul(*turning[child], *steps[child])
            values = [a + c for a, c in zip(*terms)]
            if not last:
                inside = jnp.abs(waves[2 * k, 4] + float(8 * m)) < NR / 2
                values = [jnp.where(inside, value, 0.0) for value in values]
            for part, value in enumerate(values):
                for side in range(2):
                    piece = value[:, side * LANES : (side + 1) * LANES]
                    if last:
                        final[part, side, 8 * m : 8 * m + 8] = piece
                    else:
                        images[target, side, part, 8 * m : 8 * m + 8, :] = piece

    block_of = iota((8, LANES), 1) // 16
    for part in range(2):
        for side in range(2):
            values = [final[part, side, pl.ds(i, 8, stride=8), :] for i in range(8)]
            for d in (4, 2, 1):
                clear = (block_of & d) == 0
                for i in range(8):
                    if i & d == 0:
                        a, b = values[i], values[i | d]
                        values[i] = jnp.where(clear, a, pltpu.roll(b, 16 * d, 1))
                        values[i | d] = jnp.where(clear, pltpu.roll(a, LANES - 16 * d, 1), b)
            for q in range(8):
                at = (side * 8 + q) ^ PASS_FIRST
                out_ref[at, part * 8 : part * 8 + 8, :] = values[q]


def invert_kernel(data, mixer_ref, out_ref):
    mixer = mixer_ref[...]
    for i in range(8):
        high, low = split(data[pl.ds(i, 2 * PASSES, stride=8), :])
        right_side = jnp.concatenate([high, low, high, jnp.zeros_like(high)], axis=0)
        tomo = jnp.dot(mixer, right_side.astype(BF16), preferred_element_type=F32)
        real, imag = tomo[:HEIGHTS], tomo[HEIGHTS:]
        out_ref[pl.ds(i, HEIGHTS, stride=8), :] = real * real + imag * imag


VMEM = pl.BlockSpec(memory_space=pltpu.VMEM)
HBM = pl.BlockSpec(memory_space=pltpu.HBM)
LIMIT = 16 << 20


def exchange(array, axis, first):
    members = [i ^ first for i in range(lax.axis_size(axis))]
    return lax.all_to_all(array, axis, 0, 0, axis_index_groups=[members], tiled=True)


def in_hbm(array):
    return pltpu.with_memory_space_constraint(array, pltpu.HBM)


def body(
    echo,
    chirp,
    pair_swap,
    range_shift,
    angle_shift,
    range_taps,
    angle_taps,
    phase_rates,
    invert,
    baseline_index,
):
    tables = (
        pair_swap,
        jnp.transpose(range_shift, (0, 2, 1)),
        jnp.transpose(angle_shift, (0, 2, 3, 1)),
        range_taps,
        angle_taps,
        jnp.transpose(phase_rates, (1, 2, 3, 0)),
    )
    tables = [in_hbm(table) for table in tables]
    held = [pltpu.SMEM(table.shape, table.dtype) for table in tables]
    params = pltpu.CompilerParams(vmem_limit_bytes=LIMIT)
    blocks = pl.pallas_call(
        compress_kernel,
        name="compress",
        out_shape=jax.ShapeDtypeStruct((N_AP // QUARTERS, QUARTERS, 2 * PULSES, LANES), F32),
        in_specs=[HBM] * 8,
        out_specs=HBM,
        scratch_shapes=[
            pltpu.VMEM((PULSES, 2, NS), BF16),
            pltpu.VMEM((2, TAPS), BF16),
            pltpu.VMEM((2 * PULSES, NS), F32),
            pltpu.VMEM((2, 2 * PULSES * BLOCKS, LANES), F32),
            pltpu.VMEM((2 * PULSES, 24 + BLOCKS, LANES), F32),
            pltpu.VMEM((2 * PULSES * FRAME_ROWS, LANES), F32),
            pltpu.VMEM((2, 2, TILES, PULSES, LANES), F32),
            pltpu.VMEM((QUARTERS, N_AP // QUARTERS, 2 * PULSES, LANES), F32),
            *held,
            pltpu.SemaphoreType.DMA((8 + QUARTERS,)),
        ],
        compiler_params=params,
        cost_estimate=pl.CostEstimate(flops=10**8, bytes_accessed=10**6, transcendentals=0),
    )(in_hbm(echo), in_hbm(chirp), *tables)
    weights, waves, taps, mixer = pl.pallas_call(
        tables_kernel,
        name="tables",
        out_shape=(
            jax.ShapeDtypeStruct((2 * CROSS, 2 * LANES, 2 * LANES), BF16),
            jax.ShapeDtypeStruct((2 * CROSS, 5, 8, 2 * LANES), F32),
            jax.ShapeDtypeStruct((2 * CROSS, KT, 8, LANES), F32),
            jax.ShapeDtypeStruct((2 * HEIGHTS, LANES), BF16),
        ),
        in_specs=[HBM] * 8,
        out_specs=(VMEM,) * 4,
        scratch_shapes=[
            pltpu.VMEM((2, BASES, HEIGHTS), F32),
            pltpu.SMEM((PASSES,), jnp.int32),
            *held,
            pltpu.SemaphoreType.DMA((8,)),
        ],
        compiler_params=params,
        cost_estimate=pl.CostEstimate(flops=10**8, bytes_accessed=10**6, transcendentals=0),
    )(*tables, in_hbm(jnp.transpose(invert, (0, 2, 1))), in_hbm(baseline_index))
    blocks = blocks.reshape(N_AP, 2 * PULSES, LANES)
    blocks = exchange(blocks, "ap", AP_FIRST)
    stacks = pl.pallas_call(
        merge_kernel,
        name="merge",
        out_shape=jax.ShapeDtypeStruct((PASSES, 16, LANES), F32),
        in_specs=[VMEM] * 4,
        out_specs=VMEM,
        scratch_shapes=[
            pltpu.VMEM((2, 2, 2, LANES, LANES), F32),
            pltpu.VMEM((2, 2, RW, LANES), F32),
        ],
        compiler_params=params,
        cost_estimate=pl.CostEstimate(flops=10**8, bytes_accessed=10**6, transcendentals=0),
    )(blocks, weights, waves, taps)
    stacks = exchange(stacks, "pass", PASS_FIRST)
    power = pl.pallas_call(
        invert_kernel,
        name="invert",
        out_shape=jax.ShapeDtypeStruct((HEIGHTS * 8, LANES), F32),
        in_specs=[VMEM, VMEM],
        out_specs=VMEM,
        compiler_params=params,
        cost_estimate=pl.CostEstimate(flops=10**8, bytes_accessed=10**6, transcendentals=0),
    )(stacks.reshape(PASSES * 16, LANES), mixer)
    return power.reshape(1, HEIGHTS, 1, RW * BEAMS // PASSES)


def solution(mesh):
    return jax.shard_map(
        body,
        mesh=mesh,
        in_specs=(
            P("pass", "ap", None, None),
            P(),
            P("pass", None),
            P("pass", None, None),
            P("pass", None, None, None),
            P(),
            P(),
            P(),
            P(),
            P(),
        ),
        out_specs=P("pass", None, "ap", None),
        check_vma=False,
    )
```

```python
import math

import jax
import jax.numpy as jnp
from jax import lax
from jax.experimental import pallas as pl
from jax.experimental.pallas import tpu as pltpu
from jax.sharding import PartitionSpec as P

NR = 2048
TAPS = 1024
NS = 3072
HEIGHTS = 64
KT = 8
ORIGIN = KT // 2 - 1
RMAX = 16
BASES = 32
LEVELS = 8
LOCAL = 3
CROSS = 5
PULSES = 8
N_AP = 32
PASSES = 16
RW = 64
QUARTERS = 4
AP_FIRST = 20
PASS_FIRST = 12
BEAMS = 256
LANES = 128
TILES = 17
BLOCKS = NR // LANES
FRAME_ROWS = 24
WINDOW = TAPS + LANES
SQRT_HALF = math.sqrt(0.5)
F32 = jnp.float32
BF16 = jnp.bfloat16

ROWS = (96, 88, 80, 72, 64)
FIRST_ROW = tuple(sum(ROWS[:k]) for k in range(CROSS))


def iota(shape, dim):
    return lax.broadcasted_iota(jnp.int32, shape, dim)


def sincos(x):
    turns = jnp.floor(x * (2.0 / math.pi) + 0.5)
    quadrant = turns.astype(jnp.int32)
    y = x - turns * 1.5703125
    y = y - turns * 4.837512969970703e-4
    y = y - turns * 7.54978995489188e-8
    y2 = y * y
    s = y * (1.0 + y2 * (-1.6666654611e-1 + y2 * (8.3321608736e-3 + y2 * -1.9515295891e-4)))
    c = 1.0 - 0.5 * y2 + y2 * y2 * (4.166664568298827e-2 + y2 * (-1.388731625493765e-3 + y2 * 2.443315711809948e-5))
    swap = (quadrant & 1) == 1
    cos_abs = jnp.where(swap, s, c)
    sin_abs = jnp.where(swap, c, s)
    cos = jnp.where(((quadrant + 1) & 2) == 2, -cos_abs, cos_abs)
    sin = jnp.where((quadrant & 2) == 2, -sin_abs, sin_abs)
    return cos, sin


def complex_mul(ar, ai, br, bi):
    return ar * br - ai * bi, ar * bi + ai * br


def reverse_bits(value):
    result = 0
    for digit in range(CROSS):
        result = result + (value // 2**digit % 2) * 2 ** (CROSS - 1 - digit)
    return result


def role(tables, level, child):
    flip = tables[0][0, level]
    return flip if child == 0 else 1 - flip


def step_offset(tables, level, child):
    return tables[1][0, role(tables, level, child), level] - ORIGIN


def slope_and_bend(tables, level, e, parity):
    rates = tables[5]
    slope = jnp.where(parity == 1, rates[e, 1, 0, level], rates[e, 0, 0, level])
    bend = jnp.where(parity == 1, rates[e, 1, 1, level], rates[e, 0, 1, level])
    return slope * (8.0 / NR), 8.0 * bend


def split(value):
    high = value.astype(BF16).astype(F32)
    return high, value - high


def start_copies(sources, targets, arrived):
    copies = [
        pltpu.make_async_copy(source, target, arrived.at[i])
        for i, (source, target) in enumerate(zip(sources, targets))
    ]
    for copy in copies:
        copy.start()
    return copies


def compress_kernel(
    echo_ref,
    chirp_ref,
    swap_ref,
    range_shift_ref,
    angle_shift_ref,
    range_taps_ref,
    angle_taps_ref,
    rates_ref,
    out_ref,
    echo,
    chirp,
    echo_rows,
    product,
    shifting,
    framed,
    images,
    outgoing,
    *scalars,
):
    *tables, arrived = scalars
    fetch_chirp = pltpu.make_async_copy(chirp_ref, chirp, arrived.at[len(tables)])
    fetch_chirp.start()
    fetch = pltpu.make_async_copy(echo_ref.at[0], echo, arrived.at[len(tables) + 1])
    fetch.start()
    fetch_tables = start_copies(
        (
            swap_ref,
            range_shift_ref,
            angle_shift_ref,
            range_taps_ref,
            angle_taps_ref,
            rates_ref,
        ),
        tables,
        arrived,
    )
    _, _, angle_shift_ref, range_taps_ref, angle_taps_ref, _ = tables
    rows8 = iota((PULSES, LANES), 0)
    lanes8 = iota((PULSES, LANES), 1)

    fetch_chirp.wait()
    bands = []
    row = iota((LANES, LANES), 0)
    column = iota((LANES, LANES), 1)
    for part in range(2):
        previous = jnp.zeros((LANES, LANES), F32)
        pieces = []
        for t in range(WINDOW // LANES):
            if t * LANES < TAPS:
                samples = chirp[part : part + 1, t * LANES : (t + 1) * LANES].astype(F32)
                current = pltpu.roll(
                    jnp.broadcast_to(samples, (LANES, LANES)), 0, 1, stride=1, stride_axis=0
                )
            else:
                current = jnp.zeros((LANES, LANES), F32)
            pieces.append(jnp.where(column >= row, current, previous).astype(BF16))
            previous = current
        bands.append(jnp.concatenate(pieces, axis=1))
    banded = jnp.concatenate(bands, axis=0)

    shifting[:, :8] = jnp.zeros((2 * PULSES, 8, LANES), F32)
    shifting[:, 8 + BLOCKS :] = jnp.zeros((2 * PULSES, 16, LANES), F32)

    fetch.wait()
    for n in range(PULSES):
        echo_rows[2 * n : 2 * n + 2, :] = echo[n].astype(F32)
    signal = echo_rows[...].astype(BF16)
    windows = jnp.concatenate(
        [signal[:, b * LANES : b * LANES + WINDOW] for b in range(BLOCKS)], axis=0
    )
    correlated = lax.dot_general(
        windows, banded, (((1,), (1,)), ((), ())), preferred_element_type=F32
    )
    for part in range(2):
        product[part] = correlated[:, part * LANES : (part + 1) * LANES]

    for copy in fetch_tables:
        copy.wait()

    position = lax.axis_index("ap")
    offset_above = jnp.int32(0)
    for level in range(LOCAL, LEVELS):
        bit = position // 2 ** (level - LOCAL) % 2
        offset_above = offset_above + jnp.where(
            bit == 1, step_offset(tables, level, 1), step_offset(tables, level, 0)
        )
    local_steps = [
        [step_offset(tables, level, child) for child in range(2)] for level in range(LOCAL)
    ]

    def prepare(level):
        beams = 2**level
        roles = [role(tables, level, child) for child in range(2)]
        in_child = rows8 >> level & 1
        tap_rows = [
            jnp.where(
                in_child == 1,
                range_taps_ref[level, roles[1], u],
                range_taps_ref[level, roles[0], u],
            )
            for u in range(KT)
        ]

        row16 = iota((2 * PULSES, LANES), 0)
        lane16 = iota((2 * PULSES, LANES), 1)
        of_child = row16 >> 3
        row_out = row16 & 7
        parity16 = row16 & 1

        def of_row(pick):
            return jnp.where(
                of_child == 1,
                jnp.where(parity16 == 1, pick(roles[1], 1), pick(roles[1], 0)),
                jnp.where(parity16 == 1, pick(roles[0], 1), pick(roles[0], 0)),
            )

        shift = of_row(lambda e, h: angle_shift_ref[0, e, h, level])
        beam = row_out % (2 * beams) // 2
        first = (row_out // (2 * beams) * 2 + of_child) * beams
        weights = jnp.zeros((2 * PULSES, LANES), F32)
        for u in range(KT):
            picked = first + jnp.clip(beam + (u - ORIGIN) + shift, 0, beams - 1)
            tap = of_row(lambda e, h: angle_taps_ref[level, e, h, u])
            weights = weights + jnp.where((lane16 & 7) == picked, tap, 0.0)
        high, low = split(weights)
        piece = lane16 >> 3
        left_side = jnp.where(piece < 2, high, jnp.where(piece == 2, low, 0.0)).astype(BF16)[:, :32]

        offset_out = jnp.full((PULSES, LANES), offset_above, jnp.int32)
        for later in range(level + 1, LOCAL):
            offset_out = offset_out + jnp.where(
                (rows8 >> later & 1) == 1, local_steps[later][1], local_steps[later][0]
            )
        cell_out = offset_out + lanes8
        beam_fraction = (rows8 % (2 * beams)).astype(F32) / (2.0 * beams)
        waves = []
        steps = []
        for child in range(2):
            slope, bend = slope_and_bend(tables, level, roles[child], rows8 & 1)
            cos, sin = sincos(slope * cell_out.astype(F32) + bend * beam_fraction)
            waves.append((cos * SQRT_HALF, sin * SQRT_HALF))
            steps.append(sincos(slope * float(LANES)))

        return tap_rows, left_side, cell_out, waves, steps

    totals = []
    for n in range(PULSES):
        total = offset_above
        for level in range(LOCAL):
            total = total + local_steps[level][n >> level & 1]
        totals.append(total)
        rest = total & (LANES - 1)
        even, odd = (
            [product[part, pl.ds(2 * n + i, BLOCKS, stride=16), :] for part in range(2)]
            for i in range(2)
        )
        for part, value in enumerate((even[0] + odd[1], odd[0] - even[1])):
            shifting[2 * n + part, 8 : 8 + BLOCKS] = pltpu.roll(
                value, (LANES - rest) & (LANES - 1), 1
            )
    lane = iota((FRAME_ROWS, LANES), 1)
    for n in range(PULSES):
        whole = totals[n] >> 7
        keep = lane < LANES - (totals[n] & (LANES - 1))
        for part in range(2):
            i = 2 * n + part
            left = shifting[i, pl.ds(8 + whole, FRAME_ROWS), :]
            right = shifting[i, pl.ds(9 + whole, FRAME_ROWS), :]
            framed[i * FRAME_ROWS : (i + 1) * FRAME_ROWS] = jnp.where(keep, left, right)

    sends = []

    def send(window, values):
        block = reverse_bits(window) ^ AP_FIRST
        for part in range(2):
            outgoing[block % QUARTERS, block // QUARTERS, part * 8 : part * 8 + 8] = values[part]
        if (window + 1) % (N_AP // QUARTERS) == 0:
            quarter = block % QUARTERS
            sends.append(
                pltpu.make_async_copy(
                    outgoing.at[quarter], out_ref.at[:, quarter], arrived.at[8 + quarter]
                )
            )
            sends[-1].start()

    def load(level, part, b):
        if level == 0:
            return framed[pl.ds(part * FRAME_ROWS + b, PULSES, stride=2 * FRAME_ROWS), :]
        return images[level % 2, part, b]

    for level in range(LOCAL):
        tap_rows, left_side, cell_out, waves, steps = prepare(level)

        def turn(value, cells):
            return pltpu.roll(value, LANES - cells, 1)

        def moved(here, there, cells):
            return jnp.where(lanes8 < LANES - cells, here, there)

        def rolls(b):
            values = [load(level, part, b) for part in range(2)]
            return [[value] + [turn(value, u) for u in (1, 2, 3)] for value in values]

        def runs(here, there):
            found = []
            for part in range(2):
                value = here[part][0]
                near, far = tap_rows[0] * value, tap_rows[4] * value
                for u in (1, 2, 3):
                    value = moved(here[part][u], there[part][u], u)
                    near = near + tap_rows[u] * value
                    far = far + tap_rows[4 + u] * value
                found.append((near, turn(far, 4)))
            return found

        here = rolls(0)
        there = rolls(1)
        sums = runs(here, there)
        for b in range(TILES):
            if b + 1 < TILES:
                here, there = there, rolls(b + 2) if b + 2 < TILES else there
                sums_there = runs(here, there)
            pieces = []
            for part in range(2):
                total = sums[part][0] + moved(sums[part][1], sums_there[part][1], 4)
                high, low = split(total)
                pieces.append(
                    jnp.concatenate([high, low, high, jnp.zeros((PULSES, LANES), F32)], axis=0)
                )
            sums = sums_there
            right_side = jnp.concatenate(pieces, axis=1).astype(BF16)
            steered = jnp.dot(left_side, right_side, preferred_element_type=F32)
            terms = []
            for child in range(2):
                rows = steered[child * PULSES : (child + 1) * PULSES]
                terms.append(complex_mul(*waves[child], rows[:, :LANES], rows[:, LANES:]))
                waves[child] = complex_mul(*waves[child], *steps[child])
            values = [a + c for a, c in zip(*terms)]
            if b * LANES < LEVELS * (RMAX + ORIGIN) or (b + 1) * LANES > NR - LEVELS * RMAX:
                where_r = cell_out + b * LANES
                inside = (where_r >= 0) & (where_r < NR)
                values = [jnp.where(inside, value, 0.0) for value in values]
            if level + 1 < LOCAL:
                for part in range(2):
                    images[(level + 1) % 2, part, b] = values[part]
            else:
                turned = [pltpu.roll(value, RW, 1) for value in values]
                if b > 0:
                    joined = [jnp.where(lanes8 < RW, a, c) for a, c in zip(before, turned)]
                    send(2 * b - 1, joined)
                if b < BLOCKS:
                    send(2 * b, values)
                before = turned
    for copy in sends:
        copy.wait()


def column_offset(tables, level, column):
    offset = jnp.zeros_like(column)
    for later in range(level + 1, LEVELS):
        bit = column >> (7 - (later - level - 1)) & 1
        offset = offset + jnp.where(
            bit == 1, step_offset(tables, later, 1), step_offset(tables, later, 0)
        )
    return offset


def tables_kernel(
    swap_ref,
    range_shift_ref,
    angle_shift_ref,
    range_taps_ref,
    angle_taps_ref,
    rates_ref,
    invert_ref,
    baseline_ref,
    weights_ref,
    waves_ref,
    taps_ref,
    mixer_ref,
    invert,
    baseline,
    *scalars,
):
    *tables, arrived = scalars
    for copy in start_copies(
        (
            swap_ref,
            range_shift_ref,
            angle_shift_ref,
            range_taps_ref,
            angle_taps_ref,
            rates_ref,
            invert_ref,
            baseline_ref,
        ),
        (*tables, invert, baseline),
        arrived,
    ):
        copy.wait()
    _, _, angle_shift_ref, range_taps_ref, angle_taps_ref, _ = tables
    position = lax.axis_index("ap")
    base = reverse_bits(position) * RW
    column = iota((1, 2 * LANES), 1)
    row = iota((LANES, 2 * LANES), 0)
    parity = column & 1
    for k in range(CROSS):
        level = LOCAL + k
        first_wave = FIRST_ROW[k]
        beams = 2**level
        beam = column % (2 * beams) // 2
        first_row = column // (2 * beams) * beams
        beam_fraction = (column % (2 * beams)).astype(F32) / (2.0 * beams)
        cell = iota((8, 2 * LANES), 0) + (base + column_offset(tables, level, column))
        centred = cell.astype(F32) - (NR - 1) / 2
        for child in range(2):
            e = role(tables, level, child)
            shift = jnp.where(
                parity == 1, angle_shift_ref[0, e, 1, level], angle_shift_ref[0, e, 0, level]
            )
            weights = jnp.zeros((LANES, 2 * LANES), F32)
            for u in range(KT):
                tap = jnp.where(
                    parity == 1, angle_taps_ref[level, e, 1, u], angle_taps_ref[level, e, 0, u]
                )
                picked = first_row + jnp.clip(beam + (u - ORIGIN) + shift, 0, beams - 1)
                weights = weights + jnp.where(row == picked, tap, 0.0)
            high, low = split(weights)
            at = 2 * k + child
            weights_ref[at, :LANES] = high.astype(BF16)
            weights_ref[at, LANES:] = low.astype(BF16)
            slope, bend = slope_and_bend(tables, level, e, parity)
            cos, sin = sincos(slope * cell.astype(F32) + bend * beam_fraction)
            wave = (cos * SQRT_HALF, sin * SQRT_HALF)
            step = sincos(jnp.broadcast_to(slope * 8.0, (8, 2 * LANES)))
            for m in range(ROWS[k] // 8):
                inside = jnp.abs(centred + float(8 * m)) < NR / 2
                for part in range(2):
                    waves_ref[child, part, first_wave + 8 * m : first_wave + 8 * m + 8] = (
                        jnp.where(inside, wave[part], 0.0)
                    )
                wave = complex_mul(*wave, *step)
            for u in range(KT):
                taps_ref[at, u : u + 1] = jnp.full((1, LANES), range_taps_ref[level, e, u], F32)

    lane = iota((1, LANES), 1)
    wanted = jnp.zeros((1, LANES), jnp.int32)
    for p in range(PASSES):
        wanted = jnp.where(lane % (2 * PASSES) // 2 == p ^ PASS_FIRST, baseline[p], wanted)
    chosen = (iota((BASES, LANES), 0) == wanted).astype(F32)
    steer = [
        lax.dot_general(
            invert[part],
            chosen,
            (((0,), (0,)), ((), ())),
            precision=lax.Precision.HIGHEST,
            preferred_element_type=F32,
        )
        for part in range(2)
    ]
    imaginary = (lane & 1) == 1
    high, low = split(
        jnp.concatenate(
            [jnp.where(imaginary, -steer[1], steer[0]), jnp.where(imaginary, steer[0], steer[1])],
            axis=0,
        )
    )
    piece = lane // (2 * PASSES)
    mixer_ref[...] = jnp.where(piece < 2, high, jnp.where(piece == 2, low, 0.0)).astype(BF16)


def merge_kernel(
    blocks,
    weights,
    waves,
    taps,
    out_ref,
    images,
    final,
):
    for child in range(2):
        order = []
        for i in range(N_AP // 2):
            order.append(
                child + 2 * (i >> 3 & 1) + 4 * (i >> 2 & 1) + 8 * (i >> 1 & 1) + 16 * (i & 1)
            )
        for part in range(2):
            stacked = jnp.concatenate(
                [blocks[g ^ AP_FIRST, part * PULSES : (part + 1) * PULSES, :] for g in order], axis=0
            )
            images[0, child, part] = stacked.T

    for k in range(CROSS):
        rows = ROWS[k]
        source, target = k % 2, 1 - k % 2
        last = k == CROSS - 1
        steered = []
        for child in range(2):
            tap = [
                jnp.broadcast_to(taps[2 * k + child, u : u + 1], (rows, LANES)) for u in range(KT)
            ]
            parts = []
            for part in range(2):
                total = tap[0] * images[source, child, part, 0:rows, :]
                for u in range(1, KT):
                    total = total + tap[u] * images[source, child, part, u : u + rows, :]
                parts.append(total)
            ranged = jnp.concatenate(parts, axis=0)
            high = ranged.astype(BF16)
            low = (ranged - high.astype(F32)).astype(BF16)
            matrix = weights[2 * k + child]
            steered.append(
                jnp.dot(
                    jnp.concatenate([high, low, high], axis=1),
                    jnp.concatenate([matrix[:LANES], matrix[:LANES], matrix[LANES:]], axis=0),
                    preferred_element_type=F32,
                )
            )
        for m in range(rows // 8):
            at = FIRST_ROW[k] + 8 * m
            terms = [
                complex_mul(
                    waves[child, 0, at : at + 8],
                    waves[child, 1, at : at + 8],
                    steered[child][8 * m : 8 * m + 8],
                    steered[child][rows + 8 * m : rows + 8 * m + 8],
                )
                for child in range(2)
            ]
            values = [a + c for a, c in zip(*terms)]
            for part, value in enumerate(values):
                for side in range(2):
                    piece = value[:, side * LANES : (side + 1) * LANES]
                    if last:
                        final[part, side, 8 * m : 8 * m + 8] = piece
                    else:
                        images[target, side, part, 8 * m : 8 * m + 8, :] = piece

    block_of = iota((8, LANES), 1) // 16
    for part in range(2):
        for side in range(2):
            values = [final[part, side, pl.ds(i, 8, stride=8), :] for i in range(8)]
            for d in (4, 2, 1):
                clear = (block_of & d) == 0
                for i in range(8):
                    if i & d == 0:
                        a, b = values[i], values[i | d]
                        values[i] = jnp.where(clear, a, pltpu.roll(b, 16 * d, 1))
                        values[i | d] = jnp.where(clear, pltpu.roll(a, LANES - 16 * d, 1), b)
            for q in range(8):
                at = (side * 8 + q) ^ PASS_FIRST
                out_ref[at, part * 8 : part * 8 + 8, :] = values[q]


def invert_kernel(data, mixer_ref, out_ref):
    mixer = mixer_ref[...]
    for i in range(8):
        high, low = split(data[pl.ds(i, 2 * PASSES, stride=8), :])
        right_side = jnp.concatenate([high, low, high, jnp.zeros_like(high)], axis=0)
        tomo = jnp.dot(mixer, right_side.astype(BF16), preferred_element_type=F32)
        real, imag = tomo[:HEIGHTS], tomo[HEIGHTS:]
        out_ref[pl.ds(i, HEIGHTS, stride=8), :] = real * real + imag * imag


VMEM = pl.BlockSpec(memory_space=pltpu.VMEM)
HBM = pl.BlockSpec(memory_space=pltpu.HBM)
LIMIT = 16 << 20


def exchange(array, axis, first):
    members = [i ^ first for i in range(lax.axis_size(axis))]
    return lax.all_to_all(array, axis, 0, 0, axis_index_groups=[members], tiled=True)


def in_hbm(array):
    return pltpu.with_memory_space_constraint(array, pltpu.HBM)


def body(
    echo,
    chirp,
    pair_swap,
    range_shift,
    angle_shift,
    range_taps,
    angle_taps,
    phase_rates,
    invert,
    baseline_index,
):
    tables = (
        pair_swap,
        jnp.transpose(range_shift, (0, 2, 1)),
        jnp.transpose(angle_shift, (0, 2, 3, 1)),
        range_taps,
        angle_taps,
        jnp.transpose(phase_rates, (1, 2, 3, 0)),
    )
    tables = [in_hbm(table) for table in tables]
    held = [pltpu.SMEM(table.shape, table.dtype) for table in tables]
    params = pltpu.CompilerParams(vmem_limit_bytes=LIMIT)
    blocks = pl.pallas_call(
        compress_kernel,
        name="compress",
        out_shape=jax.ShapeDtypeStruct((N_AP // QUARTERS, QUARTERS, 2 * PULSES, LANES), F32),
        in_specs=[HBM] * 8,
        out_specs=HBM,
        scratch_shapes=[
            pltpu.VMEM((PULSES, 2, NS), BF16),
            pltpu.VMEM((2, TAPS), BF16),
            pltpu.VMEM((2 * PULSES, NS), F32),
            pltpu.VMEM((2, 2 * PULSES * BLOCKS, LANES), F32),
            pltpu.VMEM((2 * PULSES, 24 + BLOCKS, LANES), F32),
            pltpu.VMEM((2 * PULSES * FRAME_ROWS, LANES), F32),
            pltpu.VMEM((2, 2, TILES, PULSES, LANES), F32),
            pltpu.VMEM((QUARTERS, N_AP // QUARTERS, 2 * PULSES, LANES), F32),
            *held,
            pltpu.SemaphoreType.DMA((8 + QUARTERS,)),
        ],
        compiler_params=params,
        cost_estimate=pl.CostEstimate(flops=10**8, bytes_accessed=10**6, transcendentals=0),
    )(in_hbm(echo), in_hbm(chirp), *tables)
    weights, waves, taps, mixer = pl.pallas_call(
        tables_kernel,
        name="tables",
        out_shape=(
            jax.ShapeDtypeStruct((2 * CROSS, 2 * LANES, 2 * LANES), BF16),
            jax.ShapeDtypeStruct((2, 2, sum(ROWS), 2 * LANES), F32),
            jax.ShapeDtypeStruct((2 * CROSS, KT, LANES), F32),
            jax.ShapeDtypeStruct((2 * HEIGHTS, LANES), BF16),
        ),
        in_specs=[HBM] * 8,
        out_specs=(VMEM,) * 4,
        scratch_shapes=[
            pltpu.VMEM((2, BASES, HEIGHTS), F32),
            pltpu.SMEM((PASSES,), jnp.int32),
            *held,
            pltpu.SemaphoreType.DMA((8,)),
        ],
        compiler_params=params,
        cost_estimate=pl.CostEstimate(flops=10**8, bytes_accessed=10**6, transcendentals=0),
    )(*tables, in_hbm(jnp.transpose(invert, (0, 2, 1))), in_hbm(baseline_index))
    blocks = blocks.reshape(N_AP, 2 * PULSES, LANES)
    blocks = exchange(blocks, "ap", AP_FIRST)
    stacks = pl.pallas_call(
        merge_kernel,
        name="merge",
        out_shape=jax.ShapeDtypeStruct((PASSES, 16, LANES), F32),
        in_specs=[VMEM] * 4,
        out_specs=VMEM,
        scratch_shapes=[
            pltpu.VMEM((2, 2, 2, LANES, LANES), F32),
            pltpu.VMEM((2, 2, RW, LANES), F32),
        ],
        compiler_params=params,
        cost_estimate=pl.CostEstimate(flops=10**8, bytes_accessed=10**6, transcendentals=0),
    )(blocks, weights, waves, taps)
    stacks = exchange(stacks, "pass", PASS_FIRST)
    power = pl.pallas_call(
        invert_kernel,
        name="invert",
        out_shape=jax.ShapeDtypeStruct((HEIGHTS * 8, LANES), F32),
        in_specs=[VMEM, VMEM],
        out_specs=VMEM,
        compiler_params=params,
        cost_estimate=pl.CostEstimate(flops=10**8, bytes_accessed=10**6, transcendentals=0),
    )(stacks.reshape(PASSES * 16, LANES), mixer)
    return power.reshape(1, HEIGHTS, 1, RW * BEAMS // PASSES)


def solution(mesh):
    return jax.shard_map(
        body,
        mesh=mesh,
        in_specs=(
            P("pass", "ap", None, None),
            P(),
            P("pass", None),
            P("pass", None, None),
            P("pass", None, None, None),
            P(),
            P(),
            P(),
            P(),
            P(),
        ),
        out_specs=P("pass", None, "ap", None),
        check_vma=False,
    )
```
